32 devices in a mesh: grp: 4 (over z), ch: 8 (over y, x, core).
Axes of the slice: x: 2, y: 2, z: 4, core: 2. Of those that a mesh axis runs over, the one named last changes fastest.
Arguments:
- features: bfloat16 [64, 64, 512], P(('grp', 'ch')), may hold values from -6 to 6
- live_counts: int32 [32], P(('grp', 'ch')), may hold values from 1 to 2, as said below
- neighbours: int32 [64, 27], P(('grp', 'ch')), may hold values from -1 to 63, as said below
- w_first: bfloat16 [27, 64, 64], replicated, may hold values from -0.21875 to 0.21875
- w_second: bfloat16 [27, 64, 64], replicated, may hold values from -0.21875 to 0.21875
- w_middle: bfloat16 [27, 128, 64], replicated, may hold values from -0.3125 to 0.3125
- w_coarse: bfloat16 [27, 256, 128], P(None, 'ch'), may hold values from -0.21875 to 0.21875
- w_project: bfloat16 [256, 64], P('ch'), may hold values from -0.75 to 0.75
- w_output: bfloat16 [64, 128], replicated, may hold values from -0.5 to 0.5
Outputs:
- mixed_out: bfloat16 [64, 64, 512], P(('grp', 'ch'))
The draws below stay inside these ranges and needn't reach their ends.
Inputs may be any that keep to these rules, and one draw needn't show every extreme that they name: Device d holds its live blocks in slots d * 2 to d * 2 + live_counts[d] - 1; the rest are padding. In every group of devices along ch one device holds exactly 2. `neighbours`: the live blocks occupy distinct positions of a lattice of 16 x 16 x (2 times the size of grp) positions; the devices with grp index g hold exactly the blocks of layers g * 2 to (g + 1) * 2 - 1 along z. Within a group, the device with ch index m (of n) holds blocks only in the tile of x from floor(2 m / n) * 8 to that plus 16 / 2 - 1 and y from (m mod (n / 2)) * 2 * 16 / n to that plus 2 * 16 / n - 1. For a live block b, entry 9 (dx + 1) + 3 (dy + 1) + dz + 1 is the block at b's position plus (dx, dy, dz), or -1 where that position is empty or off the lattice; entry 13 is b itself. Rows of padding slots are all -1, and no entry names a padding slot.
All inputs are finite; a program needn't handle non-finite values.
Results may differ from the reference program's by a relative error of at most 0.013.
Values may be sent and summed in bfloat16 or wider, within the bound.
A program may use at most 128 MiB of HBM per device.

```python
import jax
import jax.numpy as jnp
from jax import lax

C0 = 64
C1 = 128
C2 = 256
EDGE = 8
SIDE = 16
LAYERS = 2
BLK_DEV = 2
GROUP_BLOCKS = 16
BLOCKS = 64


def scene(key):
    base_key = jax.random.fold_in(key, 11)
    counts_key, choose_key, order_key = jax.random.split(base_key, 3)
    groups = BLOCKS // GROUP_BLOCKS
    members = GROUP_BLOCKS // BLK_DEV
    places = SIDE * SIDE * LAYERS
    tile_size = places // members
    half_members = members // 2
    tile_x = SIDE // 2
    tile_y = SIDE // half_members
    lowest = max(BLK_DEV // 2, 1)
    counts = jax.random.randint(counts_key, (groups, members), lowest, BLK_DEV + 1)
    fullest = jax.random.randint(choose_key, (groups, 1), 0, members)
    counts = jnp.where(jnp.arange(members)[None, :] == fullest, BLK_DEV, counts).astype(jnp.int32)
    member_keys = jax.random.split(order_key, groups * members)
    orders = jax.vmap(lambda one_key: jax.random.permutation(one_key, tile_size))(member_keys)
    local = orders.reshape(groups, members, tile_size)[:, :, :BLK_DEV].astype(jnp.int32)
    slot_index = jnp.arange(BLK_DEV, dtype=jnp.int32)[None, None, :]
    member_ids = jnp.arange(members, dtype=jnp.int32)[None, :, None]
    group_ids = jnp.arange(groups, dtype=jnp.int32)[:, None, None]
    living = slot_index < counts[:, :, None]
    coord_x = member_ids // half_members * tile_x + local // (tile_y * LAYERS)
    coord_y = member_ids % half_members * tile_y + local // LAYERS % tile_y
    coord_z = local % LAYERS + group_ids * LAYERS
    place_all = coord_z // LAYERS * places + coord_x * SIDE * LAYERS + coord_y * LAYERS + coord_z % LAYERS
    ids = group_ids * GROUP_BLOCKS + member_ids * BLK_DEV + slot_index
    target = jnp.where(living, place_all, groups * places).reshape(-1)
    block_id = jnp.full((groups * places,), -1, jnp.int32).at[target].set(ids.reshape(-1).astype(jnp.int32), mode='drop')
    columns = []
    for shift_x in (-1, 0, 1):
        for shift_y in (-1, 0, 1):
            for shift_z in (-1, 0, 1):
                next_x = coord_x + shift_x
                next_y = coord_y + shift_y
                next_z = coord_z + shift_z
                inside = (next_x >= 0) & (next_x < SIDE) & (next_y >= 0) & (next_y < SIDE) & (next_z >= 0) & (next_z < groups * LAYERS)
                place = next_z // LAYERS * places + next_x * SIDE * LAYERS + next_y * LAYERS + next_z % LAYERS
                found = jnp.take(block_id, jnp.clip(place, 0, groups * places - 1))
                columns.append(jnp.where(inside & living, found, -1))
    table = jnp.stack(columns, axis=-1).reshape(BLOCKS, 27).astype(jnp.int32)
    return (counts.reshape(-1), table)


def draw_live_counts(key, part):
    return scene(key)[0]


def draw_neighbours(key, part):
    return scene(key)[1]


def steps_of(own_key, shape, pieces, low, high):
    loudness = 1.0
    for axis_at, blocks in pieces:
        heights = jax.random.uniform(jax.random.fold_in(jax.random.fold_in(own_key, 6), axis_at), (blocks,), jnp.float32, low / len(pieces), high / len(pieces))
        loudness = loudness * jnp.repeat(jnp.exp(heights), shape[axis_at] // blocks).reshape((-1,) + (1,) * (len(shape) - 1 - axis_at))
    return loudness


def normal_values(stream_key, extent, width, reach, cuts=(), kind=jnp.bfloat16):
    level = steps_of(stream_key, extent, cuts, -0.22, 0.18) if cuts else 1.0
    values = jax.random.normal(stream_key, extent, jnp.float32) * width * level
    return jnp.minimum(jnp.maximum(values, -reach), reach).astype(kind)


def setup_inputs(seed: int = 0) -> dict:
    splits = jax.random.split(jax.random.key(seed), 10)
    features = normal_values(splits[0], (BLOCKS, C0, EDGE ** 3), 1.0, 6.0, ((0, 32),))
    live_counts = draw_live_counts(jax.random.fold_in(splits[9], 71), 0)
    neighbours = draw_neighbours(jax.random.fold_in(splits[9], 71), 0)
    w_first = normal_values(splits[3], (27, C0, C0), (27 * C0 // 2) ** -0.5, 0.21875)
    w_second = normal_values(splits[4], (27, C0, C0), (27 * C0 // 2) ** -0.5, 0.21875)
    w_middle = normal_values(splits[5], (27, C1, C0), (27 * C0 // 4) ** -0.5, 0.3125)
    w_coarse = normal_values(splits[6], (27, C2, C1), (27 * C1 // 4) ** -0.5, 0.21875, ((1, 8),))
    w_project = normal_values(splits[7], (C2, C0), (C2 // 4) ** -0.5, 0.75, ((0, 8),))
    w_output = normal_values(splits[8], (C0, 2 * C0), (2 * C0) ** -0.5, 0.5)
    return dict(features=features, live_counts=live_counts, neighbours=neighbours, w_first=w_first, w_second=w_second, w_middle=w_middle, w_coarse=w_coarse, w_project=w_project, w_output=w_output)


offsets = [(shift_x, shift_y, shift_z) for shift_x in (-1, 0, 1) for shift_y in (-1, 0, 1) for shift_z in (-1, 0, 1)]


def ranges_for(step_in, margin, length):
    if step_in < 0:
        return 0, margin, length - margin, length
    if step_in == 0:
        return margin, margin + length, 0, length
    return margin + length, length + 2 * margin, 0, margin


def extend(volume, neighbour_rows, margin):
    count_rows = neighbour_rows.shape[0]
    channels = volume.shape[1]
    length = volume.shape[2]
    side_out = length + 2 * margin
    result = jnp.zeros((count_rows, channels, side_out, side_out, side_out), jnp.float32)
    for column, (shift_x, shift_y, shift_z) in enumerate(offsets):
        target = neighbour_rows[:, column]
        safe_rows = jnp.clip(target, 0, volume.shape[0] - 1)
        low_x, high_x, from_x, till_x = ranges_for(shift_x, margin, length)
        low_y, high_y, from_y, till_y = ranges_for(shift_y, margin, length)
        low_z, high_z, from_z, till_z = ranges_for(shift_z, margin, length)
        portion = volume[safe_rows, :, from_x:till_x, from_y:till_y, from_z:till_z]
        portion = jnp.where((target >= 0)[:, None, None, None, None], portion, jnp.zeros_like(portion))
        result = result.at[:, :, low_x:high_x, low_y:high_y, low_z:high_z].set(portion)
    return result


def convolve(padded, weight):
    inside = padded.shape[2] - 2
    summed = None
    for column, (shift_x, shift_y, shift_z) in enumerate(offsets):
        window = padded[:, :, 1 + shift_x:1 + shift_x + inside, 1 + shift_y:1 + shift_y + inside, 1 + shift_z:1 + shift_z + inside]
        product_term = jnp.einsum("oc,bcxyz->boxyz", weight[column].astype(jnp.float32), window, precision=lax.Precision.HIGHEST)
        summed = product_term if summed is None else summed + product_term
    return summed


def layer(volume, neighbours, weight, batches):
    grouped = neighbours.reshape(batches, -1, 27)

    def one_batch(neighbour_rows):
        return jax.nn.gelu(convolve(extend(volume, neighbour_rows, 1), weight)).astype(jnp.bfloat16)

    output = lax.map(one_batch, grouped)
    return output.reshape((volume.shape[0],) + output.shape[2:])


def pooled(volume):
    count_rows, channels, length = volume.shape[0], volume.shape[1], volume.shape[2]
    halved = length // 2
    blocked = volume.astype(jnp.float32).reshape(count_rows, channels, halved, 2, halved, 2, halved, 2)
    return (jnp.sum(blocked, axis=(3, 5, 7)) * 0.125).astype(jnp.bfloat16)


def reference(features, live_counts, neighbours, w_first, w_second, w_middle, w_coarse, w_project, w_output):
    batches = BLOCKS // GROUP_BLOCKS
    volume = features.reshape(BLOCKS, C0, EDGE, EDGE, EDGE).astype(jnp.float32)
    first_out = layer(volume, neighbours, w_first, batches)
    second = layer(first_out.astype(jnp.float32), neighbours, w_second, batches)
    middle_in = pooled(second)
    middle = layer(middle_in.astype(jnp.float32), neighbours, w_middle, batches)
    coarse_in = pooled(middle)
    hidden = layer(coarse_in.astype(jnp.float32), neighbours, w_coarse, batches)
    coarse = jnp.einsum("ko,bkxyz->boxyz", w_project.astype(jnp.float32), hidden.astype(jnp.float32), precision=lax.Precision.HIGHEST).astype(jnp.bfloat16)
    factor = EDGE // coarse.shape[2]
    widened = jnp.repeat(jnp.repeat(jnp.repeat(coarse, factor, axis=2), factor, axis=3), factor, axis=4)
    skipped = jnp.einsum("oc,bcxyz->boxyz", w_output[:, :C0].astype(jnp.float32), second.astype(jnp.float32), precision=lax.Precision.HIGHEST)
    lifted = jnp.einsum("oc,bcxyz->boxyz", w_output[:, C0:].astype(jnp.float32), widened.astype(jnp.float32), precision=lax.Precision.HIGHEST)
    mixed_out = skipped + lifted
    slot_ids = jnp.arange(BLOCKS, dtype=jnp.int32)
    living = (slot_ids % BLK_DEV) < live_counts[slot_ids // BLK_DEV]
    mixed_out = jnp.where(living[:, None, None, None, None], mixed_out, jnp.zeros_like(mixed_out))
    return mixed_out.astype(jnp.bfloat16).reshape(BLOCKS, C0, EDGE ** 3)
```

```python
import functools

import jax
import jax.numpy as jnp
from jax import lax
from jax.experimental import pallas as pl
from jax.experimental.pallas import tpu as pltpu
from jax.sharding import PartitionSpec as P

MESH = pl.DeviceIdType.MESH
F32, BF16 = jnp.float32, jnp.bfloat16
STEPS = (-1, 0, 1)
OFFSETS = [(x, y, z) for x in STEPS for y in STEPS for z in STEPS]
PARTNERS = [(h, y, z) for h in (0, 1) for y in STEPS for z in STEPS if (h, y, z) != (0, 0, 0)]
PIECES = 3


def matmul_nt(left, right):
    return lax.dot_general(left, right, (((1,), (1,)), ((), ())), preferred_element_type=F32)


def rounded_gelu(value):
    return jax.nn.gelu(value).astype(BF16)


def kernel(grps, n, feat_any, live_any, neigh_any, w1_any, w2_any, wm_any, wc_any, wp_any, wo_any, out, levels, mats, live, neigh, sems):
    g, m = lax.axis_index("grp"), lax.axis_index("ch")
    q = n // 2
    half, tile = m // q, m % q
    slots, c0, voxels = feat_any.shape
    edge = round(voxels ** (1 / 3))
    c1 = wm_any.shape[2]

    def has(partner):
        _, y, z = partner
        return (tile + y >= 0) & (tile + y < q) & (g + z >= 0) & (g + z < grps)

    def coords(partner):
        h, y, z = partner
        return g + z, ((1 - half) if h else half) * q + tile + y

    barrier = pltpu.get_barrier_semaphore()
    for r in range(1, n):
        pl.semaphore_signal(barrier, inc=1, device_id=(g, (m + r) % n), device_id_type=MESH)
    far = [p for p in PARTNERS if p[2] != 0]
    for p in far:

        @pl.when(has(p))
        def _():
            pl.semaphore_signal(barrier, inc=1, device_id=coords(p), device_id_type=MESH)

    (feat, w1, w2, wm, wo, wc, wp, b1, b2, bm, im_leaf, im_mid, im_coarse) = mats
    (local_sem, wsend, wrecv, psend, precv) = sems
    loads = [
        pltpu.make_async_copy(source, target, local_sem.at[i])
        for i, (source, target) in enumerate(
            [(w1_any, w1), (w2_any, w2), (wm_any, wm), (wo_any, wo), (wc_any, wc.at[m]), (wp_any, wp.at[m]), (live_any, live), (neigh_any, neigh), (feat_any, feat)]
        )
    ]
    for load in loads[-1:] + loads[:-1]:
        load.start()

    def piece_of(level, partner):
        h, y, z = partner
        volume, caps = level["v"], level["caps"]
        length = volume.shape[0]
        pick_x = pl.ds((1 - half) * (length - 1), 1) if h else slice(None)
        pick_y = slice(None) if y == 0 else (pl.ds(length - 1, 1) if y > 0 else pl.ds(0, 1))
        if z == 0:
            return volume.at[pick_x, pick_y]
        return caps.at[1 if z > 0 else 0, pick_x, pick_y]

    def copy_to(level, index):
        h, y, z = PARTNERS[index]
        back = PARTNERS.index((h, -y, -z))
        return pltpu.make_async_remote_copy(
            src_ref=piece_of(level, PARTNERS[index]),
            dst_ref=level["got"][back],
            send_sem=level["send"].at[index],
            recv_sem=level["recv"].at[back],
            device_id=coords(PARTNERS[index]),
            device_id_type=MESH,
        )

    order = sorted(range(len(PARTNERS)), key=lambda i: -sum(abs(s) for s in PARTNERS[i]))

    def caps_of(level):
        volume, caps = level["v"], level["caps"]
        length = volume.shape[0]
        caps[0] = volume[:, :, 0:1, :]
        caps[1] = volume[:, :, length - 1 : length, :]

    def send(level):
        for i in order:

            @pl.when(has(PARTNERS[i]))
            def _():
                copy_to(level, i).start()

    def receive(level):
        for i in order:
            h, y, z = PARTNERS[i]

            @pl.when(has((h, -y, -z)))
            def _():
                copy_to(level, i).wait_recv()

    def extend(level):
        volume, ext, caps = level["v"], level["ext"], level["caps"]
        length, lanes = volume.shape[0], volume.shape[3]
        middle = lanes // 2
        lane = lax.broadcasted_iota(jnp.int32, (1, 1, 1, lanes), 3)
        upper = (lane >= middle).astype(jnp.int32)
        ext[1 : length + 1, 1 : length + 1, 1 : length + 1, :] = volume[...]
        firsts = {}
        for p in [(0, 0, 0)] + PARTNERS:
            a, b = coords(p)
            firsts[p] = jnp.where(has(p), (a * n + b) * 2, -8)

        def source_at(step):
            return slice(0, length) if step == 0 else (slice(0, 1) if step > 0 else slice(length - 1, length))

        def target_at(step):
            return slice(1, length + 1) if step == 0 else (slice(0, 1) if step < 0 else slice(length + 1, length + 2))

        for column, (x, y, z) in enumerate(OFFSETS):
            if (x, y, z) == (0, 0, 0):
                continue
            wanted = jnp.where(upper == 1, neigh[1, column], neigh[0, column])
            shape = tuple(length if s == 0 else 1 for s in (x, y, z)) + (lanes,)
            wanted = jnp.broadcast_to(wanted, shape)
            upper_full = jnp.broadcast_to(upper, shape)
            value = jnp.zeros(shape, F32)
            for h in (0, 1) if x else (0,):
                for cy in (0, y) if y else (0,):
                    for cz in (0, z) if z else (0,):
                        p = (h, cy, cz)
                        at_x = slice(0, 1) if h else source_at(x)
                        at_y = slice(0, 1) if cy else source_at(y)
                        at_z = slice(0, 1) if cz else source_at(z)
                        if p == (0, 0, 0):
                            if z:
                                found = caps[0 if z > 0 else 1, at_x, at_y, :, :]
                            else:
                                found = volume[at_x, at_y, at_z, :]
                        else:
                            found = level["got"][PARTNERS.index(p)][at_x, at_y, at_z, :]
                        swapped = jnp.concatenate([found[..., middle:], found[..., :middle]], axis=3)
                        value = jnp.where(
                            wanted == firsts[p] + upper_full,
                            found,
                            jnp.where(wanted == firsts[p] + 1 - upper_full, swapped, value),
                        )
            ext[target_at(x), target_at(y), target_at(z), :] = value

    taps = wc.shape[1]

    pairs = n // 2
    pair, core = m // 2, m % 2
    partner = pair * 2 + 1 - core

    def weight_copies(part, role, r):
        first, last = taps * part // PIECES, taps * (part + 1) // PIECES
        other = (pair + pairs - r) % pairs * 2
        owner, came = [(m, partner), (m, other + core), (other + core, other + 1 - core)][role]
        target = (pair + r) % pairs * 2 + core if role == 1 else partner
        lane = (0, r, pairs - 1 + r)[role]

        def copy(who):
            spot = wc.at[who, pl.ds(first, last - first)]
            return pltpu.make_async_remote_copy(
                src_ref=spot,
                dst_ref=spot,
                send_sem=wsend.at[part, lane],
                recv_sem=wrecv.at[part, lane],
                device_id=(g, target),
                device_id_type=MESH,
            )

        return functools.partial(copy, owner), functools.partial(copy, came)

    def project_copy(r, other):
        return pltpu.make_async_remote_copy(
            src_ref=wp.at[other],
            dst_ref=wp.at[other],
            send_sem=psend.at[r - 1],
            recv_sem=precv.at[r - 1],
            device_id=(g, (m + r) % n),
            device_id_type=MESH,
        )

    def send_weights(part):
        for r in range(1, pairs):
            weight_copies(part, 1, r)[0]().start()
        weight_copies(part, 0, 0)[0]().start()

    def hand_on(part):
        for r in range(1, pairs):
            weight_copies(part, 1, r)[1]().wait_recv()
            weight_copies(part, 2, r)[0]().start()

    def diagonal(matrix):
        empty = jnp.zeros_like(matrix)
        return jnp.concatenate([matrix, empty], axis=1), jnp.concatenate([empty, matrix], axis=1)

    def fill_diagonal(weights, target):
        rows, width = weights.shape[1], 2 * weights.shape[2]
        for t in range(weights.shape[0]):
            top, bottom = diagonal(weights[t])
            at = (t % 9) * width
            target[t // 9, 0:rows, at : at + width] = top
            target[t // 9, rows : 2 * rows, at : at + width] = bottom

    def fill_upright(weights, target):
        rows, width = weights.shape[1:]
        for t in range(weights.shape[0]):
            empty = jnp.zeros((rows, width), BF16)
            for b in range(slots):
                at = (t % 9 * slots + b) * rows
                for other in range(slots):
                    there = weights[t] if other == b else empty
                    target[t // 9, at : at + rows, other * width : (other + 1) * width] = there

    def convolve_leaf(level, weights):
        ext, length, lanes = level["ext"], edge, level["v"].shape[3]
        for k in range(9):
            y, z = k // 3, k % 3
            rows = ext[:, y : y + length, z : z + length, :].reshape(length + 2, length * length, lanes)
            im_leaf[:, :, k * lanes : (k + 1) * lanes] = rows.astype(BF16)
        total = None
        for x in range(3):
            window = im_leaf[x : x + length].reshape(length**3, 9 * lanes)
            term = matmul_nt(window, weights[x])
            total = term if total is None else total + term
        return rounded_gelu(total)

    leaf_a, leaf_b, mid, low = levels
    loads[-1].wait()
    packed = feat[...].reshape(slots * c0, voxels).astype(F32)
    leaf_a["v"][...] = packed.T.reshape(edge, edge, edge, slots * c0)
    caps_of(leaf_a)
    peers = n - 1
    for p in far:
        peers = peers + has(p).astype(jnp.int32)
    pl.semaphore_wait(barrier, peers)

    send(leaf_a)
    loads[0].wait()
    fill_diagonal(w1, b1)
    loads[4].wait()
    loads[5].wait()
    send_weights(0)
    for r in range(1, n):
        project_copy(r, m).start()
    receive(leaf_a)
    loads[6].wait()
    loads[7].wait()
    extend(leaf_a)
    first = convolve_leaf(leaf_a, b1)

    leaf_b["v"][...] = first.astype(F32).reshape(edge, edge, edge, slots * c0)
    caps_of(leaf_b)
    send(leaf_b)
    send_weights(1)
    loads[1].wait()
    fill_diagonal(w2, b2)
    hand_on(0)
    receive(leaf_b)
    extend(leaf_b)
    second = convolve_leaf(leaf_b, b2)

    def halving(length):
        small = length // 2
        row = lax.broadcasted_iota(jnp.int32, (small**3, length**3), 0)
        column = lax.broadcasted_iota(jnp.int32, (small**3, length**3), 1)
        x, y, z = column // (length * length), column // length % length, column % length
        hit = row == (x // 2) * small * small + (y // 2) * small + z // 2
        return jnp.where(hit, 0.125, 0.0).astype(BF16)

    side = edge // 2
    pooled = jnp.dot(halving(edge), second, preferred_element_type=F32).astype(BF16).astype(F32)
    for x in range(side):
        for y in range(side):
            at = (x * side + y) * side
            mid["v"][x, y] = pooled[at : at + side]
    caps_of(mid)
    send(mid)
    send_weights(2)
    loads[2].wait()
    fill_upright(wm, bm)
    hand_on(1)
    receive(mid)
    extend(mid)
    lanes = slots * c0
    for k in range(9):
        ty, tz = k // 3, k % 3
        for y in range(side):
            im_mid[:, y * side : (y + 1) * side, k * lanes : (k + 1) * lanes] = mid["ext"][:, y + ty, tz : tz + side, :]
    total = None
    for x in range(3):
        window = im_mid[x : x + side].astype(BF16).reshape(side**3, 9 * lanes)
        term = jnp.dot(window, bm[x], preferred_element_type=F32)
        total = term if total is None else total + term
    middle = rounded_gelu(total)

    small = side // 2
    pooled = jnp.dot(halving(side), middle, preferred_element_type=F32).astype(BF16).astype(F32)
    for x in range(small):
        for y in range(small):
            at = (x * small + y) * small
            low["v"][x, y] = pooled[at : at + small]
    caps_of(low)
    send(low)
    loads[3].wait()
    skip_top, skip_bottom = diagonal(wo[:, :c0])
    lift_top, lift_bottom = diagonal(wo[:, c0:])
    skip_weights = jnp.concatenate([skip_top, skip_bottom], axis=0)
    lift_weights = jnp.concatenate([lift_top, lift_bottom], axis=0)
    mixed = matmul_nt(skip_weights, second)
    hand_on(2)
    for part in range(PIECES):
        weight_copies(part, 0, 0)[1]().wait_recv()
        for r in range(1, pairs):
            weight_copies(part, 2, r)[1]().wait_recv()
    for r in range(1, n):
        project_copy(r, (m + n - r) % n).wait_recv()
    receive(low)
    extend(low)
    cells = small**3
    for t in range(taps):
        tx, ty, tz = t // 9, t // 3 % 3, t % 3
        for b in range(slots):
            for x in range(small):
                for y in range(small):
                    at = b * cells + (x * small + y) * small
                    im_coarse[at : at + small, t * c1 : (t + 1) * c1] = low["ext"][
                        x + tx, y + ty, tz : tz + small, b * c1 : (b + 1) * c1
                    ]
    total = None
    c2 = n * wc.shape[2]
    for t in range(taps):
        term = matmul_nt(im_coarse[:, t * c1 : (t + 1) * c1].astype(BF16), wc[:, t].reshape(c2, c1))
        total = term if total is None else total + term
    hidden = rounded_gelu(total)
    coarse = jnp.dot(hidden, wp[...].reshape(c2, c0), preferred_element_type=F32)
    coarse = jnp.concatenate([coarse[b * cells : (b + 1) * cells] for b in range(slots)], axis=1).astype(BF16)
    row = lax.broadcasted_iota(jnp.int32, (voxels, cells), 0)
    column = lax.broadcasted_iota(jnp.int32, (voxels, cells), 1)
    factor = edge // small
    x, y, z = row // (edge * edge), row // edge % edge, row % edge
    spread = column == (x // factor) * small * small + (y // factor) * small + z // factor
    spread = jnp.where(spread, 1.0, 0.0).astype(BF16)
    widened = jnp.dot(spread, coarse, preferred_element_type=F32).astype(BF16)
    mixed = mixed + matmul_nt(lift_weights, widened)
    owner = lax.broadcasted_iota(jnp.int32, mixed.shape, 0) // c0
    mixed = jnp.where(owner < live[0], mixed, 0.0).astype(BF16)
    for b in range(slots):
        out[b] = mixed[b * c0 : (b + 1) * c0]

    for level in levels:
        for i in order:

            @pl.when(has(PARTNERS[i]))
            def _():
                copy_to(level, i).wait_send()

    for r in range(1, n):
        project_copy(r, m).wait_send()
    for part in range(PIECES):
        weight_copies(part, 0, 0)[0]().wait_send()
        for r in range(1, pairs):
            weight_copies(part, 1, r)[0]().wait_send()
            weight_copies(part, 2, r)[0]().wait_send()


def level_scratch(length, lanes):
    def got(partner):
        h, y, z = partner
        return pltpu.VMEM((1 if h else length, 1 if y else length, 1 if z else length, lanes), F32)

    return dict(
        v=pltpu.VMEM((length, length, length, lanes), F32),
        caps=pltpu.VMEM((2, length, length, 1, lanes), F32),
        ext=pltpu.VMEM((length + 2,) * 3 + (lanes,), F32),
        got=[got(p) for p in PARTNERS],
        send=pltpu.SemaphoreType.DMA((len(PARTNERS),)),
        recv=pltpu.SemaphoreType.DMA((len(PARTNERS),)),
    )


def shards(grps, n, features, live_counts, neighbours, w_first, w_second, w_middle, w_coarse, w_project, w_output):
    slots, c0, voxels = features.shape
    edge = round(voxels ** (1 / 3))
    w_middle = jnp.swapaxes(w_middle, 1, 2)
    taps, _, c1 = w_middle.shape
    lanes = slots * c0
    side, small = edge // 2, edge // 4
    levels = [
        level_scratch(edge, lanes),
        level_scratch(edge, lanes),
        level_scratch(side, lanes),
        level_scratch(small, slots * c1),
    ]
    mats = [
        pltpu.VMEM(features.shape, BF16),
        pltpu.VMEM(w_first.shape, BF16),
        pltpu.VMEM(w_second.shape, BF16),
        pltpu.VMEM(w_middle.shape, BF16),
        pltpu.VMEM(w_output.shape, BF16),
        pltpu.VMEM((n,) + w_coarse.shape, BF16),
        pltpu.VMEM((n,) + w_project.shape, BF16),
        pltpu.VMEM((3, lanes, 9 * lanes), BF16),
        pltpu.VMEM((3, lanes, 9 * lanes), BF16),
        pltpu.VMEM((3, 9 * lanes, slots * c1), BF16),
        pltpu.VMEM((edge + 2, edge * edge, 9 * lanes), BF16),
        pltpu.VMEM((side + 2, side * side, 9 * lanes), F32),
        pltpu.VMEM((slots * small**3, taps * c1), F32),
    ]
    sems = [
        pltpu.SemaphoreType.DMA((9,)),
        pltpu.SemaphoreType.DMA((PIECES, n - 1)),
        pltpu.SemaphoreType.DMA((PIECES, n - 1)),
        pltpu.SemaphoreType.DMA((n - 1,)),
        pltpu.SemaphoreType.DMA((n - 1,)),
    ]
    smem = pl.BlockSpec(memory_space=pltpu.SMEM)
    vmem = pl.BlockSpec(memory_space=pltpu.VMEM)
    stay = pl.BlockSpec(memory_space=pl.ANY)
    return pl.pallas_call(
        functools.partial(kernel, grps, n),
        out_shape=pltpu.VMEM(features.shape, BF16),
        in_specs=[stay] * 9,
        out_specs=vmem,
        scratch_shapes=[levels, mats, pltpu.SMEM(live_counts.shape, jnp.int32), pltpu.SMEM(neighbours.shape, jnp.int32), sems],
        compiler_params=pltpu.CompilerParams(collective_id=0, has_side_effects=True),
    )(features, live_counts, neighbours, w_first, w_second, w_middle, w_coarse, w_project, w_output)


def solution(mesh):
    in_specs = (
        P(("grp", "ch"), None, None),
        P(("grp", "ch")),
        P(("grp", "ch"), None),
        P(),
        P(),
        P(),
        P(None, "ch", None),
        P("ch", None),
        P(),
    )
    return jax.shard_map(
        functools.partial(shards, mesh.shape["grp"], mesh.shape["ch"]),
        mesh=mesh,
        in_specs=in_specs,
        out_specs=P(("grp", "ch"), None, None),
        check_vma=False,
    )
```

```python
import functools

import numpy as np

import jax
import jax.numpy as jnp
from jax import lax
from jax.experimental import pallas as pl
from jax.experimental.pallas import tpu as pltpu
from jax.sharding import PartitionSpec as P

MESH = pl.DeviceIdType.MESH
F32, BF16 = jnp.float32, jnp.bfloat16
STEPS = (-1, 0, 1)
OFFSETS = [(x, y, z) for x in STEPS for y in STEPS for z in STEPS]
PARTNERS = [(h, y, z) for h in (0, 1) for y in STEPS for z in STEPS if (h, y, z) != (0, 0, 0)]
PIECES = 3


def matmul_nt(left, right):
    return lax.dot_general(left, right, (((1,), (1,)), ((), ())), preferred_element_type=F32)


def rounded_gelu(value):
    return jax.nn.gelu(value).astype(BF16)


def kernel(grps, n, feat_any, live_any, neigh_any, w1_any, w2_any, wm_any, wc_any, wp_any, wo_any, table_any, out, levels, mats, live, neigh, sems):
    g, m = lax.axis_index("grp"), lax.axis_index("ch")
    q = n // 2
    half, place_y = m // q, m % q
    slots, c0, voxels = feat_any.shape
    edge = round(voxels ** (1 / 3))
    c1 = wm_any.shape[2]

    def has(partner):
        _, y, z = partner
        return (place_y + y >= 0) & (place_y + y < q) & (g + z >= 0) & (g + z < grps)

    def coords(partner):
        h, y, z = partner
        return g + z, ((1 - half) if h else half) * q + place_y + y

    barrier = pltpu.get_barrier_semaphore()
    far = [p for p in PARTNERS if p[2] != 0]
    for p in sorted(far, key=lambda p: -sum(abs(s) for s in p)):

        @pl.when(has(p))
        def _():
            pl.semaphore_signal(barrier, inc=1, device_id=coords(p), device_id_type=MESH)

    for r in range(1, n):
        pl.semaphore_signal(barrier, inc=1, device_id=(g, (m + r) % n), device_id_type=MESH)

    (feat, w1, w2, wm, wo, wc, wp, b1, b2, f1, f2, bm, im_leaf, im_mid, table, gather, ext_leaf, planes, acc) = mats
    (local_sem, wsend, wrecv, hsend, hrecv) = sems
    for i, level in enumerate(levels):
        level.update(send=hsend.at[i % 2], recv=hrecv.at[i % 2])
    loads = [
        pltpu.make_async_copy(source, target, local_sem.at[i])
        for i, (source, target) in enumerate(
            [(w1_any, w1), (w2_any, w2), (wm_any, wm), (wo_any, wo), (wc_any, wc.at[m, pl.ds(0, wc_any.shape[0])]), (wp_any, wp), (live_any, live), (neigh_any, neigh), (table_any, table), (feat_any, feat)]
        )
    ]
    for load in loads[-1:] + loads[:-1]:
        load.start()

    tile = 2 * edge
    area = edge * edge

    def leaf_piece(level, partner):
        h, y, z = partner
        upper, right = (1 if z > 0 else 0), (1 if y > 0 else 0)
        far_side = 1 - half
        if z:
            if y:
                return level["send_l"].at[upper, right]
            if h:
                return level["send_z"].at[upper, pl.ds(pl.multiple_of(far_side * (area - tile), tile), tile)]
            return level["send_z"].at[upper]
        if not h:
            return level["send_y"].at[right]
        start, size = far_side * (edge - 1) * area + right * (area - tile if y else 0), tile if y else area
        return level["flat"].at[pl.ds(pl.multiple_of(start, tile), size)]

    def unpack(level, partner):
        h, y, z = partner
        index = PARTNERS.index(partner)
        value = level["land"][index][...].astype(F32)
        target = level["got"][index]
        if value.shape[0] > tile:
            target[...] = value.reshape(target.shape)
        elif y and z:
            target[...] = value[:edge]
        elif y:
            target[0] = value[edge:] if y < 0 else value[:edge]
        else:
            target[...] = jnp.where(half == 0, value[:edge], value[edge:])

    def piece_of(level, partner):
        if "lines" in level:
            return leaf_piece(level, partner)
        if "rows" in level:
            return level["rows"]
        h, y, z = partner
        volume, caps = level["v"], level["caps"]
        length = volume.shape[0]
        pick_x = pl.ds((1 - half) * (length - 1), 1) if h else slice(None)
        pick_y = slice(None) if y == 0 else (pl.ds(length - 1, 1) if y > 0 else pl.ds(0, 1))
        if z == 0:
            return volume.at[pick_x, pick_y]
        return caps.at[1 if z > 0 else 0, pick_x, pick_y]

    def copy_to(level, index):
        h, y, z = PARTNERS[index]
        back = PARTNERS.index((h, -y, -z))
        return pltpu.make_async_remote_copy(
            src_ref=piece_of(level, PARTNERS[index]),
            dst_ref=level["got"].at[back] if "rows" in level else level.get("land", level["got"])[back],
            send_sem=level["send"].at[index],
            recv_sem=level["recv"].at[back],
            device_id=coords(PARTNERS[index]),
            device_id_type=MESH,
        )

    order = sorted(range(len(PARTNERS)), key=lambda i: -sum(abs(s) for s in PARTNERS[i]))

    def caps_of(level):
        volume, caps = level["v"], level["caps"]
        length = volume.shape[0]
        caps[0] = volume[:, :, 0:1, :]
        caps[1] = volume[:, :, length - 1 : length, :]

    def send(level):
        for i in order:

            @pl.when(has(PARTNERS[i]))
            def _():
                copy_to(level, i).start()

    order_of = [PARTNERS[i] for i in order]

    def sent(level):
        for i in order:

            @pl.when(has(PARTNERS[i]))
            def _():
                copy_to(level, i).wait_send()

    def wait_for(level, partners):
        for h, y, z in partners:

            @pl.when(has((h, -y, -z)))
            def _():
                copy_to(level, PARTNERS.index((h, y, z))).wait_recv()

    def receive(level):
        for i in order:
            h, y, z = PARTNERS[i]

            @pl.when(has((h, -y, -z)))
            def _():
                copy_to(level, i).wait_recv()

    def extend(level):
        volume, ext, caps = level["v"], level["ext"], level["caps"]
        length, lanes = volume.shape[0], volume.shape[3]
        middle = lanes // 2
        lane = lax.broadcasted_iota(jnp.int32, (1, 1, 1, lanes), 3)
        upper = (lane >= middle).astype(jnp.int32)
        ext[1 : length + 1, 1 : length + 1, 1 : length + 1, :] = volume[...]
        firsts = {}
        for p in [(0, 0, 0)] + PARTNERS:
            a, b = coords(p)
            firsts[p] = jnp.where(has(p), (a * n + b) * 2, -8)

        def source_at(step):
            return slice(0, length) if step == 0 else (slice(0, 1) if step > 0 else slice(length - 1, length))

        def target_at(step):
            return slice(1, length + 1) if step == 0 else (slice(0, 1) if step < 0 else slice(length + 1, length + 2))

        for column, (x, y, z) in enumerate(OFFSETS):
            if (x, y, z) == (0, 0, 0):
                continue
            wanted = jnp.where(upper == 1, neigh[1, column], neigh[0, column])
            shape = tuple(length if s == 0 else 1 for s in (x, y, z)) + (lanes,)
            wanted = jnp.broadcast_to(wanted, shape)
            upper_full = jnp.broadcast_to(upper, shape)
            value = jnp.zeros(shape, F32)
            for h in (0, 1) if x else (0,):
                for cy in (0, y) if y else (0,):
                    for cz in (0, z) if z else (0,):
                        p = (h, cy, cz)
                        at_x = slice(0, 1) if h else source_at(x)
                        at_y = slice(0, 1) if cy else source_at(y)
                        at_z = slice(0, 1) if cz else source_at(z)
                        if p == (0, 0, 0):
                            if z:
                                found = caps[0 if z > 0 else 1, at_x, at_y, :, :]
                            else:
                                found = volume[at_x, at_y, at_z, :]
                        else:
                            found = level["got"][PARTNERS.index(p)][at_x, at_y, at_z, :]
                        swapped = jnp.concatenate([found[..., middle:], found[..., :middle]], axis=3)
                        value = jnp.where(
                            wanted == firsts[p] + upper_full,
                            found,
                            jnp.where(wanted == firsts[p] + 1 - upper_full, swapped, value),
                        )
            ext[target_at(x), target_at(y), target_at(z), :] = value

    half_lanes = slots * c0 // 2
    lane = lax.broadcasted_iota(jnp.int32, (edge, slots * c0), 1)
    block_of = (lane >= half_lanes).astype(jnp.int32)
    first_of = {}
    for p in [(0, 0, 0)] + PARTNERS:
        a, b = coords(p)
        first_of[p] = jnp.where(has(p), (a * n + b) * 2, -8)

    def choose(column, rows, sources):
        wanted = jnp.where(block_of == 1, neigh[1, column], neigh[0, column])
        owner = block_of
        if rows < edge:
            wanted, owner = wanted[:rows], owner[:rows]
        value = None
        for p, found in sources:
            pieces = [found[r : r + min(rows, edge)] for r in range(0, rows, edge)]
            straight, crossed = wanted == first_of[p] + owner, wanted == first_of[p] + 1 - owner
            old = value if value is not None else [jnp.zeros_like(piece) for piece in pieces]
            value = [
                jnp.where(straight, piece, jnp.where(crossed, pltpu.roll(piece, half_lanes, 1), before))
                for piece, before in zip(pieces, old)
            ]
        return value

    def put(plane, kind, value):
        if kind == "face":
            for r, rows in enumerate(value):
                at = (r + 1) * 2 * edge + 1
                planes[plane, at : at + edge, :] = rows
            return
        axis, place = kind
        if axis == "row":
            at = place * 2 * edge + 1
            planes[plane, at : at + edge, :] = value[0]
        elif axis == "column":
            planes[plane, pl.ds(2 * edge + place, edge, stride=2 * edge), :] = value[0]
        else:
            at = place[0] * 2 * edge + place[1]
            planes[plane, at : at + 1, :] = value[0]

    def add_plane(plane, weights, where):
        parts = []
        for i in range(3):
            for j in range(3):
                rows = [planes[plane, (r + i) * 2 * edge + j : (r + i) * 2 * edge + j + edge, :] for r in range(edge)]
                parts.append(jnp.concatenate(rows, axis=0).astype(BF16))
        update = matmul_nt(jnp.concatenate(parts, axis=1), weights)
        axis, at = where
        if axis == "x":
            acc[pl.ds(at, area), :] += update
            return
        for r in range(edge):
            rows = update[r * edge : (r + 1) * edge]
            if axis == "y":
                acc[r * area + at : r * area + at + edge, :] += rows
            else:
                acc[pl.ds(r * area + at, edge, stride=edge), :] += rows

    small = edge // 4
    cells = small**3

    def fill_gather():
        sub = lax.broadcasted_iota(jnp.int32, (8, gather.shape[1] // 3), 0)
        col = lax.broadcasted_iota(jnp.int32, (8, gather.shape[1] // 3), 1)
        width = sub.shape[1]
        entries = [neigh[b, d] * cells for b in range(slots) for d in range(27)] + list(range(cells))
        blocks = []
        for start in range(0, width, 8):
            block = jnp.zeros(sub.shape, jnp.int32)
            for s, entry in enumerate(entries[start : start + 8]):
                block = jnp.where(sub == s, entry, block)
            blocks.append(block.astype(F32))
        keys = jnp.dot(table[...], jnp.concatenate(blocks, axis=0).astype(BF16), preferred_element_type=F32)
        rows = slots * cells
        for k in range(3):
            offer = jnp.full(sub.shape, -1000, jnp.int32)
            for i, p in enumerate([(0, 0, 0)] + PARTNERS):
                at = i * rows - k * width
                offer = jnp.where((col >= at) & (col < at + rows), first_of[p] * cells + col - at, offer)
            offer = jnp.broadcast_to(offer[:1].astype(F32), keys.shape)
            gather[:, k * width : (k + 1) * width] = jnp.where(keys == offer, 1.0, 0.0).astype(BF16)

    def column_of(x, y, z):
        return 9 * (x + 1) + 3 * (y + 1) + z + 1

    def halo(level, weights, faces):
        volume, caps, lines = level["v"], level["caps"], level["lines"]
        got = {p: level["got"][i] for i, p in enumerate(PARTNERS)}
        last = edge - 1
        near = lambda s: 0 if s > 0 else last
        beyond = lambda s: 0 if s < 0 else edge + 1
        flag = lambda s: 0 if s > 0 else 1
        line_y = lambda y: slice(near(y) * edge, near(y) * edge + edge)
        skip = lambda start: pl.ds(start, edge, stride=edge)

        def arrive(partners):
            wait_for(level, partners)
            for p in partners:
                unpack(level, p)

        arrive([(0, 0, -1), (0, 0, 1)])
        for z in (-1, 1):
            plane = 4 + (z > 0)
            sources = [((0, 0, 0), caps[flag(z)]), ((0, 0, z), got[0, 0, z][...])]
            put(plane, "face", choose(column_of(0, 0, z), edge * edge, sources))
            add_plane(plane, faces[plane - 2], ("z", last - near(z)))
        arrive([(0, -1, 0), (0, 1, 0)] + [(0, y, z) for y in (-1, 1) for z in (-1, 1)])
        for y in (-1, 1):
            plane = 2 + (y > 0)
            flat = got[0, y, 0].reshape(edge * edge, slots * c0)
            own = volume[:, line_y(y), :].reshape(edge * edge, slots * c0)
            sources = [((0, 0, 0), own), ((0, y, 0), flat[...])]
            put(plane, "face", choose(column_of(0, y, 0), edge * edge, sources))
            for z in (-1, 1):
                sources = [
                    ((0, 0, 0), lines[flag(z), flag(y)]),
                    ((0, y, 0), flat[skip(near(z)), :]),
                    ((0, 0, z), got[0, 0, z][skip(near(y)), :]),
                    ((0, y, z), got[0, y, z][...]),
                ]
                put(plane, ("column", beyond(z)), choose(column_of(0, y, z), edge, sources))
            add_plane(plane, faces[plane - 2], ("y", (last - near(y)) * edge))
        for x in (-1, 1):
            plane, xe = (x > 0) + 0, near(x)
            put(plane, "face", choose(column_of(x, 0, 0), edge * edge, [((0, 0, 0), volume[xe])]))
            for y in (-1, 1):
                sources = [((0, 0, 0), volume[xe, line_y(y), :]), ((0, y, 0), got[0, y, 0][xe])]
                put(plane, ("row", beyond(y)), choose(column_of(x, y, 0), edge, sources))
            for z in (-1, 1):
                span = slice(xe * edge, xe * edge + edge)
                sources = [((0, 0, 0), caps[flag(z), span, :]), ((0, 0, z), got[0, 0, z][span, :])]
                put(plane, ("column", beyond(z)), choose(column_of(x, 0, z), edge, sources))
            for y in (-1, 1):
                for z in (-1, 1):
                    at = xe * edge + near(y)
                    sources = [
                        ((0, 0, 0), lines[flag(z), flag(y), xe : xe + 1, :]),
                        ((0, y, 0), got[0, y, 0][xe, near(z) : near(z) + 1, :]),
                        ((0, 0, z), got[0, 0, z][at : at + 1, :]),
                        ((0, y, z), got[0, y, z][xe : xe + 1, :]),
                    ]
                    put(plane, ("cell", (beyond(y), beyond(z))), choose(column_of(x, y, z), 1, sources))
            add_plane(plane, weights[2 * (x > 0)], ("x", (last - xe) * edge * edge))
        arrive([p for p in order_of[::-1] if p[0] == 1])
        plane = 6
        x = 1 - 2 * half
        face = got[1, 0, 0]
        put(plane, "face", choose(column_of(x, 0, 0), edge * edge, [((1, 0, 0), face[0])]))
        for y in (-1, 1):
            sources = [((1, 0, 0), face[0, line_y(y), :]), ((1, y, 0), got[1, y, 0][0])]
            put(plane, ("row", beyond(y)), choose(column_of(x, y, 0), edge, sources))
        for z in (-1, 1):
            sources = [((1, 0, 0), face[0, skip(near(z)), :]), ((1, 0, z), got[1, 0, z][...])]
            put(plane, ("column", beyond(z)), choose(column_of(x, 0, z), edge, sources))
        for y in (-1, 1):
            for z in (-1, 1):
                at = near(y) * edge + near(z)
                sources = [
                    ((1, 0, 0), face[0, at : at + 1, :]),
                    ((1, y, 0), got[1, y, 0][0, near(z) : near(z) + 1, :]),
                    ((1, 0, z), got[1, 0, z][near(y) : near(y) + 1, :]),
                    ((1, y, z), got[1, y, z][pl.ds(half * last, 1), :]),
                ]
                put(plane, ("cell", (beyond(y), beyond(z))), choose(column_of(x, y, z), 1, sources))
        facing = pl.multiple_of((1 - half) * last * edge * edge, edge * edge)
        add_plane(plane, weights[2 * (1 - half)], ("x", facing))

    def surface(level):
        volume, caps, lines = level["v"], level["caps"], level["lines"]
        for k, z in enumerate((0, edge - 1)):
            for x in range(edge):
                caps[k, x * edge : (x + 1) * edge, :] = volume[x, pl.ds(z, edge, stride=edge), :]
            for j, y in enumerate((0, edge - 1)):
                line = caps[k, pl.ds(y, edge, stride=edge), :]
                lines[k, j] = line
                level["send_l"][k, j] = jnp.concatenate([line, line], axis=0).astype(BF16)
            level["send_z"][k] = caps[k].astype(BF16)
        for j, y in enumerate((0, edge - 1)):
            face = volume[:, y * edge : (y + 1) * edge, :].reshape(area, slots * c0)
            level["send_y"][j] = face.astype(BF16)

    def fill_faces(weights, target):
        width = slots * c0
        for k in range(2):
            for i in range(3):
                target[k, :, 3 * i * width : 3 * (i + 1) * width] = weights[i, :, 6 * k * width : (6 * k + 3) * width]
                for j in range(3):
                    at, tap = (3 * i + j) * width, (3 * j + 2 * k) * width
                    target[2 + k, :, at : at + width] = weights[i, :, tap : tap + width]

    taps = wc.shape[1] - 1

    pairs = n // 2
    pair, core = m // 2, m % 2
    partner = pair * 2 + 1 - core

    def weight_copies(part, role, r):
        first, last = (taps + 1) * part // PIECES, (taps + 1) * (part + 1) // PIECES
        other = (pair + pairs - r) % pairs * 2
        owner, came = [(m, partner), (m, other + core), (other + core, other + 1 - core)][role]
        target = (pair + r) % pairs * 2 + core if role == 1 else partner
        lane = (0, r, pairs - 1 + r)[role]

        def copy(who):
            spot = wc.at[who, pl.ds(first, last - first)]
            return pltpu.make_async_remote_copy(
                src_ref=spot,
                dst_ref=spot,
                send_sem=wsend.at[part, lane],
                recv_sem=wrecv.at[part, lane],
                device_id=(g, target),
                device_id_type=MESH,
            )

        return functools.partial(copy, owner), functools.partial(copy, came)

    def send_weights(part):
        for r in range(1, pairs):
            weight_copies(part, 1, r)[0]().start()
        weight_copies(part, 0, 0)[0]().start()

    def hand_on(part):
        for r in range(1, pairs):
            weight_copies(part, 1, r)[1]().wait_recv()
            weight_copies(part, 2, r)[0]().start()

    def diagonal(matrix):
        empty = jnp.zeros_like(matrix)
        return jnp.concatenate([matrix, empty], axis=1), jnp.concatenate([empty, matrix], axis=1)

    def fill_diagonal(weights, target):
        rows, width = weights.shape[1], 2 * weights.shape[2]
        for t in range(weights.shape[0]):
            top, bottom = diagonal(weights[t])
            at = (t % 9) * width
            target[t // 9, 0:rows, at : at + width] = top
            target[t // 9, rows : 2 * rows, at : at + width] = bottom

    def fill_upright(weights, target):
        rows, width = weights.shape[1:]
        for t in range(weights.shape[0]):
            empty = jnp.zeros((rows, width), BF16)
            for b in range(slots):
                at = (t % 9 * slots + b) * rows
                for other in range(slots):
                    there = weights[t] if other == b else empty
                    target[t // 9, at : at + rows, other * width : (other + 1) * width] = there

    def convolve_own(level, weights):
        lanes = slots * c0
        inside = slice(1, edge + 1)
        ext_leaf[inside, inside, inside, :] = level["v"][...].reshape(edge, edge, edge, lanes)
        for k in range(9):
            y, z = k // 3, k % 3
            rows = ext_leaf[:, y : y + edge, z : z + edge, :].reshape(edge + 2, edge * edge, lanes)
            im_leaf[:, :, k * lanes : (k + 1) * lanes] = rows.astype(BF16)
        total = None
        for x in range(3):
            window = im_leaf[x : x + edge].reshape(edge**3, 9 * lanes)
            term = matmul_nt(window, weights[x])
            total = term if total is None else total + term
        acc[...] = total

    leaf_a, leaf_b, mid, low = levels
    loads[-1].wait()
    packed = feat[...].reshape(slots * c0, voxels).astype(F32)
    turned = packed.T
    leaf_a["v"][...] = turned.reshape(edge, area, slots * c0)
    leaf_a["flat"][...] = turned.astype(BF16)
    surface(leaf_a)
    ext_leaf[...] = jnp.zeros_like(ext_leaf)
    planes[...] = jnp.zeros_like(planes)
    peers = n - 1
    for p in far:
        peers = peers + has(p).astype(jnp.int32)
    pl.semaphore_wait(barrier, peers)

    send(leaf_a)
    loads[4].wait()
    loads[5].wait()
    wc[m, taps] = jnp.concatenate([wp[...]] * (c1 // c0), axis=1)
    send_weights(0)
    loads[0].wait()
    fill_diagonal(w1, b1)
    fill_faces(b1, f1)
    convolve_own(leaf_a, b1)
    loads[6].wait()
    loads[7].wait()
    loads[8].wait()
    fill_gather()
    halo(leaf_a, b1, f1)
    first = rounded_gelu(acc[...])

    leaf_b["flat"][...] = first
    leaf_b["v"][...] = first.astype(F32).reshape(edge, area, slots * c0)
    surface(leaf_b)
    send(leaf_b)
    send_weights(1)
    loads[1].wait()
    fill_diagonal(w2, b2)
    fill_faces(b2, f2)
    convolve_own(leaf_b, b2)
    hand_on(0)
    sent(leaf_a)
    halo(leaf_b, b2, f2)
    second = rounded_gelu(acc[...])

    def halving(length):
        small = length // 2
        row = lax.broadcasted_iota(jnp.int32, (small**3, length**3), 0)
        column = lax.broadcasted_iota(jnp.int32, (small**3, length**3), 1)
        x, y, z = column // (length * length), column // length % length, column % length
        hit = row == (x // 2) * small * small + (y // 2) * small + z // 2
        return jnp.where(hit, 0.125, 0.0).astype(BF16)

    side = edge // 2
    pooled = jnp.dot(halving(edge), second, preferred_element_type=F32).astype(BF16).astype(F32)
    for x in range(side):
        for y in range(side):
            at = (x * side + y) * side
            mid["v"][x, y] = pooled[at : at + side]
    caps_of(mid)
    send(mid)
    send_weights(2)
    loads[2].wait()
    fill_upright(wm, bm)
    hand_on(1)
    sent(leaf_b)
    receive(mid)
    extend(mid)
    lanes = slots * c0
    for k in range(9):
        ty, tz = k // 3, k % 3
        for y in range(side):
            im_mid[:, y * side : (y + 1) * side, k * lanes : (k + 1) * lanes] = mid["ext"][:, y + ty, tz : tz + side, :]
    total = None
    for x in range(3):
        window = im_mid[x : x + side].astype(BF16).reshape(side**3, 9 * lanes)
        term = jnp.dot(window, bm[x], preferred_element_type=F32)
        total = term if total is None else total + term
    middle = rounded_gelu(total)

    pooled = jnp.dot(halving(side), middle, preferred_element_type=F32)
    pooled = jnp.concatenate([pooled[:, b * c1 : (b + 1) * c1] for b in range(slots)], axis=0).astype(BF16)
    low["rows"][...] = pooled
    send(low)
    loads[3].wait()
    skip_top, skip_bottom = diagonal(wo[:, :c0])
    lift_top, lift_bottom = diagonal(wo[:, c0:])
    skip_weights = jnp.concatenate([skip_top, skip_bottom], axis=0)
    lift_weights = jnp.concatenate([lift_top, lift_bottom], axis=0)
    mixed = matmul_nt(skip_weights, second)
    hand_on(2)
    for part in range(PIECES):
        weight_copies(part, 0, 0)[1]().wait_recv()
        for r in range(1, pairs):
            weight_copies(part, 2, r)[1]().wait_recv()
    receive(low)
    sources = [pooled]
    for i, p in enumerate(PARTNERS):
        sources.append(jnp.where(has(p), low["got"][i], jnp.zeros_like(pooled)))
    spare = gather.shape[1] - len(sources) * slots * cells
    sources.append(jnp.zeros((spare, c1), BF16))
    spread = jnp.dot(gather[...], jnp.concatenate(sources, axis=0), preferred_element_type=F32).astype(BF16)
    rows = slots * cells
    window = jnp.concatenate([spread[t * rows : (t + 1) * rows] for t in range(taps)], axis=1)
    c2 = n * wc.shape[2]
    weights = jnp.concatenate([wc[:, t].reshape(c2, c1) for t in range(taps)], axis=1)
    total = matmul_nt(window, weights)
    hidden = rounded_gelu(total)
    coarse = jnp.dot(hidden, wc[:, taps].reshape(c2, c1)[:, :c0], preferred_element_type=F32)
    coarse = jnp.concatenate([coarse[b * cells : (b + 1) * cells] for b in range(slots)], axis=1).astype(BF16)
    row = lax.broadcasted_iota(jnp.int32, (voxels, cells), 0)
    column = lax.broadcasted_iota(jnp.int32, (voxels, cells), 1)
    factor = edge // small
    x, y, z = row // (edge * edge), row // edge % edge, row % edge
    spread = column == (x // factor) * small * small + (y // factor) * small + z // factor
    spread = jnp.where(spread, 1.0, 0.0).astype(BF16)
    widened = jnp.dot(spread, coarse, preferred_element_type=F32).astype(BF16)
    mixed = mixed + matmul_nt(lift_weights, widened)
    owner = lax.broadcasted_iota(jnp.int32, mixed.shape, 0) // c0
    mixed = jnp.where(owner < live[0], mixed, 0.0).astype(BF16)
    for b in range(slots):
        out[b] = mixed[b * c0 : (b + 1) * c0]

    sent(mid)
    sent(low)
    for part in range(PIECES):
        weight_copies(part, 0, 0)[0]().wait_send()
        for r in range(1, pairs):
            weight_copies(part, 1, r)[0]().wait_send()
            weight_copies(part, 2, r)[0]().wait_send()


def leaf_scratch(length, lanes):
    def got(partner):
        h, y, z = partner
        if z == 0:
            return pltpu.VMEM((1 if h else length, length if y else length**2, lanes), F32)
        return pltpu.VMEM((length if h or y else length**2, lanes), F32)

    return dict(
        v=pltpu.VMEM((length, length**2, lanes), F32),
        caps=pltpu.VMEM((2, length**2, lanes), F32),
        lines=pltpu.VMEM((2, 2, length, lanes), F32),
        flat=pltpu.VMEM((length**3, lanes), BF16),
        send_y=pltpu.VMEM((2, length**2, lanes), BF16),
        send_z=pltpu.VMEM((2, length**2, lanes), BF16),
        send_l=pltpu.VMEM((2, 2, 2 * length, lanes), BF16),
        land=[pltpu.VMEM((length**2 if sum(map(abs, p)) == 1 else 2 * length, lanes), BF16) for p in PARTNERS],
        got=[got(p) for p in PARTNERS],
    )


def coarse_table(slots, small):
    cells = small**3
    table = np.zeros((len(OFFSETS) * slots * cells, 128), np.float32)
    row = 0
    for tap in OFFSETS:
        for b in range(slots):
            for cell in np.ndindex(small, small, small):
                there = np.array(cell) + np.array(tap)
                x, y, z = there // small + 1
                table[row, b * 27 + 9 * x + 3 * y + z] = 1
                x, y, z = there % small
                table[row, slots * 27 + (x * small + y) * small + z] = 1
                row += 1
    return jnp.asarray(table, BF16)


def level_scratch(length, lanes):
    def got(partner):
        h, y, z = partner
        return pltpu.VMEM((1 if h else length, 1 if y else length, 1 if z else length, lanes), F32)

    return dict(
        v=pltpu.VMEM((length, length, length, lanes), F32),
        caps=pltpu.VMEM((2, length, length, 1, lanes), F32),
        ext=pltpu.VMEM((length + 2,) * 3 + (lanes,), F32),
        got=[got(p) for p in PARTNERS],
    )


def shards(grps, n, features, live_counts, neighbours, w_first, w_second, w_middle, w_coarse, w_project, w_output):
    slots, c0, voxels = features.shape
    edge = round(voxels ** (1 / 3))
    w_middle = jnp.swapaxes(w_middle, 1, 2)
    taps, _, c1 = w_middle.shape
    lanes = slots * c0
    side, small = edge // 2, edge // 4
    levels = [
        leaf_scratch(edge, lanes),
        leaf_scratch(edge, lanes),
        level_scratch(side, lanes),
        dict(
            rows=pltpu.VMEM((slots * small**3, c1), BF16),
            got=pltpu.VMEM((len(PARTNERS), slots * small**3, c1), BF16),
        ),
    ]
    table = coarse_table(slots, small)
    mats = [
        pltpu.VMEM(features.shape, BF16),
        pltpu.VMEM(w_first.shape, BF16),
        pltpu.VMEM(w_second.shape, BF16),
        pltpu.VMEM(w_middle.shape, BF16),
        pltpu.VMEM(w_output.shape, BF16),
        pltpu.VMEM((n, taps + 1) + w_coarse.shape[1:], BF16),
        pltpu.VMEM(w_project.shape, BF16),
        pltpu.VMEM((3, lanes, 9 * lanes), BF16),
        pltpu.VMEM((3, lanes, 9 * lanes), BF16),
        pltpu.VMEM((4, lanes, 9 * lanes), BF16),
        pltpu.VMEM((4, lanes, 9 * lanes), BF16),
        pltpu.VMEM((3, 9 * lanes, slots * c1), BF16),
        pltpu.VMEM((edge + 2, edge * edge, 9 * lanes), BF16),
        pltpu.VMEM((side + 2, side * side, 9 * lanes), F32),
        pltpu.VMEM(table.shape, BF16),
        pltpu.VMEM((table.shape[0], 3 * 128), BF16),
        pltpu.VMEM((edge + 2,) * 3 + (lanes,), F32),
        pltpu.VMEM((7, (edge + 2) * 2 * edge, lanes), F32),
        pltpu.VMEM((edge**3, lanes), F32),
    ]
    sems = [
        pltpu.SemaphoreType.DMA((10,)),
        pltpu.SemaphoreType.DMA((PIECES, n - 1)),
        pltpu.SemaphoreType.DMA((PIECES, n - 1)),
        pltpu.SemaphoreType.DMA((2, len(PARTNERS))),
        pltpu.SemaphoreType.DMA((2, len(PARTNERS))),
    ]
    smem = pl.BlockSpec(memory_space=pltpu.SMEM)
    vmem = pl.BlockSpec(memory_space=pltpu.VMEM)
    stay = pl.BlockSpec(memory_space=pl.ANY)
    return pl.pallas_call(
        functools.partial(kernel, grps, n),
        out_shape=pltpu.VMEM(features.shape, BF16),
        in_specs=[stay] * 10,
        out_specs=vmem,
        scratch_shapes=[levels, mats, pltpu.SMEM(live_counts.shape, jnp.int32), pltpu.SMEM(neighbours.shape, jnp.int32), sems],
        compiler_params=pltpu.CompilerParams(collective_id=0, has_side_effects=True),
    )(features, live_counts, neighbours, w_first, w_second, w_middle, w_coarse, w_project, w_output, table)


def solution(mesh):
    in_specs = (
        P(("grp", "ch"), None, None),
        P(("grp", "ch")),
        P(("grp", "ch"), None),
        P(),
        P(),
        P(),
        P(None, "ch", None),
        P("ch", None),
        P(),
    )
    return jax.shard_map(
        functools.partial(shards, mesh.shape["grp"], mesh.shape["ch"]),
        mesh=mesh,
        in_specs=in_specs,
        out_specs=P(("grp", "ch"), None, None),
        check_vma=False,
    )
```

```python
import functools

import numpy as np

import jax
import jax.numpy as jnp
from jax import lax
from jax.experimental import pallas as pl
from jax.experimental.pallas import tpu as pltpu
from jax.sharding import PartitionSpec as P

MESH = pl.DeviceIdType.MESH
F32, BF16 = jnp.float32, jnp.bfloat16
STEPS = (-1, 0, 1)
OFFSETS = [(x, y, z) for x in STEPS for y in STEPS for z in STEPS]
PARTNERS = [(h, y, z) for h in (0, 1) for y in STEPS for z in STEPS if (h, y, z) != (0, 0, 0)]
PIECES = 3


def matmul_nt(left, right):
    return lax.dot_general(left, right, (((1,), (1,)), ((), ())), preferred_element_type=F32)


def rounded_gelu(value):
    return jax.nn.gelu(value).astype(BF16)


def kernel(grps, n, feat_any, live_any, neigh_any, w1_any, w2_any, wm_any, wc_any, wp_any, wo_any, table_any, out, levels, mats, live, neigh, sems):
    g, m = lax.axis_index("grp"), lax.axis_index("ch")
    q = n // 2
    half, place_y = m // q, m % q
    slots, c0, voxels = feat_any.shape
    edge = round(voxels ** (1 / 3))
    c1 = wm_any.shape[2]

    def has(partner):
        _, y, z = partner
        return (place_y + y >= 0) & (place_y + y < q) & (g + z >= 0) & (g + z < grps)

    def coords(partner):
        h, y, z = partner
        return g + z, ((1 - half) if h else half) * q + place_y + y

    barrier = pltpu.get_barrier_semaphore()
    far = [p for p in PARTNERS if p[2] != 0]
    for p in sorted(far, key=lambda p: -sum(abs(s) for s in p)):

        @pl.when(has(p))
        def _():
            pl.semaphore_signal(barrier, inc=1, device_id=coords(p), device_id_type=MESH)

    for r in range(1, n):
        pl.semaphore_signal(barrier, inc=1, device_id=(g, (m + r) % n), device_id_type=MESH)

    (feat, w1, w2, wm, wo, wc, wp, b1, b2, f1, f2, bm, im_leaf, im_mid, table, gather, ext_leaf, planes, acc) = mats
    (local_sem, wsend, wrecv, hsend, hrecv) = sems
    for i, level in enumerate(levels):
        level.update(send=hsend.at[i % 2], recv=hrecv.at[i % 2])
    loads = [
        pltpu.make_async_copy(source, target, local_sem.at[i])
        for i, (source, target) in enumerate(
            [(w1_any, w1), (w2_any, w2), (wm_any, wm), (wo_any, wo), (wc_any, wc.at[m % 2, m // 2, pl.ds(0, wc_any.shape[0])]), (wp_any, wp), (live_any, live), (neigh_any, neigh), (table_any, table), (feat_any, feat)]
        )
    ]
    for load in loads[-1:] + loads[:-1]:
        load.start()

    area = edge * edge

    def leaf_piece(level, partner):
        h, y, z = partner
        upper, right = (1 if z > 0 else 0), (1 if y > 0 else 0)
        far_side = 1 - half
        if z:
            if y:
                return level["send_l"].at[upper, right]
            if h:
                return level["send_z"].at[upper, pl.ds(pl.multiple_of(far_side * (area - edge), edge), edge)]
            return level["send_z"].at[upper]
        if not h:
            return level["send_y"].at[right]
        start, size = far_side * (edge - 1) * area + right * (area - edge if y else 0), edge if y else area
        return level["flat"].at[pl.ds(pl.multiple_of(start, edge), size)]

    def unpack(level, partner):
        index = PARTNERS.index(partner)
        value = level["land"][index][...].astype(F32)
        target = level["got"][index]
        target[...] = value.reshape(target.shape)

    def piece_of(level, partner):
        if "lines" in level:
            return leaf_piece(level, partner)
        if "rows" in level:
            return level["rows"]
        h, y, z = partner
        volume, caps = level["v"], level["caps"]
        length = volume.shape[0]
        pick_x = pl.ds((1 - half) * (length - 1), 1) if h else slice(None)
        pick_y = slice(None) if y == 0 else (pl.ds(length - 1, 1) if y > 0 else pl.ds(0, 1))
        if z == 0:
            return volume.at[pick_x, pick_y]
        return caps.at[1 if z > 0 else 0, pick_x, pick_y]

    def copy_to(level, index):
        h, y, z = PARTNERS[index]
        back = PARTNERS.index((h, -y, -z))
        return pltpu.make_async_remote_copy(
            src_ref=piece_of(level, PARTNERS[index]),
            dst_ref=level["got"].at[back] if "rows" in level else level.get("land", level["got"])[back],
            send_sem=level["send"].at[index],
            recv_sem=level["recv"].at[back],
            device_id=coords(PARTNERS[index]),
            device_id_type=MESH,
        )

    order = sorted(range(len(PARTNERS)), key=lambda i: -sum(abs(s) for s in PARTNERS[i]))

    def caps_of(level):
        volume, caps = level["v"], level["caps"]
        length = volume.shape[0]
        caps[0] = volume[:, :, 0:1, :]
        caps[1] = volume[:, :, length - 1 : length, :]

    def send(level):
        for i in order:

            @pl.when(has(PARTNERS[i]))
            def _():
                copy_to(level, i).start()

    order_of = [PARTNERS[i] for i in order]

    def sent(level):
        for i in order:

            @pl.when(has(PARTNERS[i]))
            def _():
                copy_to(level, i).wait_send()

    def wait_for(level, partners):
        for h, y, z in partners:

            @pl.when(has((h, -y, -z)))
            def _():
                copy_to(level, PARTNERS.index((h, y, z))).wait_recv()

    def receive(level):
        for i in order:
            h, y, z = PARTNERS[i]

            @pl.when(has((h, -y, -z)))
            def _():
                copy_to(level, i).wait_recv()

    def extend(level):
        volume, ext, caps = level["v"], level["ext"], level["caps"]
        length, lanes = volume.shape[0], volume.shape[3]
        middle = lanes // 2
        lane = lax.broadcasted_iota(jnp.int32, (1, 1, 1, lanes), 3)
        upper = (lane >= middle).astype(jnp.int32)
        ext[1 : length + 1, 1 : length + 1, 1 : length + 1, :] = volume[...]
        firsts = {}
        for p in [(0, 0, 0)] + PARTNERS:
            a, b = coords(p)
            firsts[p] = jnp.where(has(p), (a * n + b) * 2, -8)

        def source_at(step):
            return slice(0, length) if step == 0 else (slice(0, 1) if step > 0 else slice(length - 1, length))

        def target_at(step):
            return slice(1, length + 1) if step == 0 else (slice(0, 1) if step < 0 else slice(length + 1, length + 2))

        for column, (x, y, z) in enumerate(OFFSETS):
            if (x, y, z) == (0, 0, 0):
                continue
            wanted = jnp.where(upper == 1, neigh[1, column], neigh[0, column])
            shape = tuple(length if s == 0 else 1 for s in (x, y, z)) + (lanes,)
            wanted = jnp.broadcast_to(wanted, shape)
            upper_full = jnp.broadcast_to(upper, shape)
            value = jnp.zeros(shape, F32)
            for h in (0, 1) if x else (0,):
                for cy in (0, y) if y else (0,):
                    for cz in (0, z) if z else (0,):
                        p = (h, cy, cz)
                        at_x = slice(0, 1) if h else source_at(x)
                        at_y = slice(0, 1) if cy else source_at(y)
                        at_z = slice(0, 1) if cz else source_at(z)
                        if p == (0, 0, 0):
                            if z:
                                found = caps[0 if z > 0 else 1, at_x, at_y, :, :]
                            else:
                                found = volume[at_x, at_y, at_z, :]
                        else:
                            found = level["got"][PARTNERS.index(p)][at_x, at_y, at_z, :]
                        swapped = jnp.concatenate([found[..., middle:], found[..., :middle]], axis=3)
                        value = jnp.where(
                            wanted == firsts[p] + upper_full,
                            found,
                            jnp.where(wanted == firsts[p] + 1 - upper_full, swapped, value),
                        )
            ext[target_at(x), target_at(y), target_at(z), :] = value

    half_lanes = slots * c0 // 2
    lane = lax.broadcasted_iota(jnp.int32, (edge, slots * c0), 1)
    block_of = (lane >= half_lanes).astype(jnp.int32)
    first_of = {}
    for p in [(0, 0, 0)] + PARTNERS:
        a, b = coords(p)
        first_of[p] = jnp.where(has(p), (a * n + b) * 2, -8)

    def choose(column, rows, sources, value=None):
        wanted = jnp.where(block_of == 1, neigh[1, column], neigh[0, column])
        owner = block_of
        if rows < edge:
            wanted, owner = wanted[:rows], owner[:rows]
        for p, found in sources:
            pieces = [found[r : r + min(rows, edge)] for r in range(0, rows, edge)]
            straight, crossed = wanted == first_of[p] + owner, wanted == first_of[p] + 1 - owner
            old = value if value is not None else [jnp.zeros_like(piece) for piece in pieces]
            value = [
                jnp.where(straight, piece, jnp.where(crossed, pltpu.roll(piece, half_lanes, 1), before))
                for piece, before in zip(pieces, old)
            ]
        return value

    def spots(plane, kind):
        axis, place = kind
        pitch = 2 * edge
        if axis == "face":
            return [(plane, slice((r + 1) * pitch + 1, (r + 1) * pitch + 1 + edge)) for r in range(edge)]
        if axis == "row":
            return [(plane, slice(place * pitch + 1, place * pitch + 1 + edge))]
        if axis == "column":
            return [(plane, pl.ds(pitch + place, edge, stride=pitch))]
        return [(plane, slice(place[0] * pitch + place[1], place[0] * pitch + place[1] + 1))]

    def put(plane, kind, column, rows, sources, add=False):
        where = spots(plane, kind)
        value = choose(column, rows, sources, [planes[spot] for spot in where] if add else None)
        for spot, part in zip(where, value):
            planes[spot] = part

    def add_plane(plane, weights, where):
        parts = []
        for i in range(3):
            for j in range(3):
                rows = [planes[plane, (r + i) * 2 * edge + j : (r + i) * 2 * edge + j + edge, :] for r in range(edge)]
                parts.append(jnp.concatenate(rows, axis=0).astype(BF16))
        update = matmul_nt(jnp.concatenate(parts, axis=1), weights)
        axis, at = where
        if axis == "x":
            acc[pl.ds(at, area), :] += update
            return
        for r in range(edge):
            rows = update[r * edge : (r + 1) * edge]
            if axis == "y":
                acc[r * area + at : r * area + at + edge, :] += rows
            else:
                acc[pl.ds(r * area + at, edge, stride=edge), :] += rows

    small = edge // 4
    cells = small**3

    def fill_gather():
        sub = lax.broadcasted_iota(jnp.int32, (8, gather.shape[1] // 3), 0)
        col = lax.broadcasted_iota(jnp.int32, (8, gather.shape[1] // 3), 1)
        width = sub.shape[1]
        entries = [neigh[b, d] * cells for b in range(slots) for d in range(27)] + list(range(cells))
        blocks = []
        for start in range(0, width, 8):
            block = jnp.zeros(sub.shape, jnp.int32)
            for s, entry in enumerate(entries[start : start + 8]):
                block = jnp.where(sub == s, entry, block)
            blocks.append(block.astype(F32))
        keys = jnp.dot(table[...], jnp.concatenate(blocks, axis=0).astype(BF16), preferred_element_type=F32)
        rows = slots * cells
        for k in range(3):
            offer = jnp.full(sub.shape, -1000, jnp.int32)
            for i, p in enumerate([(0, 0, 0)] + PARTNERS):
                at = i * rows - k * width
                offer = jnp.where((col >= at) & (col < at + rows), first_of[p] * cells + col - at, offer)
            offer = jnp.broadcast_to(offer[:1].astype(F32), keys.shape)
            gather[:, k * width : (k + 1) * width] = jnp.where(keys == offer, 1.0, 0.0).astype(BF16)

    def column_of(x, y, z):
        return 9 * (x + 1) + 3 * (y + 1) + z + 1

    def halo(level, weights, faces):
        volume, caps, lines = level["v"], level["caps"], level["lines"]
        got = {p: level["got"][i] for i, p in enumerate(PARTNERS)}
        last = edge - 1
        near = lambda s: 0 if s > 0 else last
        beyond = lambda s: 0 if s < 0 else edge + 1
        flag = lambda s: 0 if s > 0 else 1
        line_y = lambda y: slice(near(y) * edge, near(y) * edge + edge)
        skip = lambda start: pl.ds(start, edge, stride=edge)

        def arrive(partners):
            wait_for(level, partners)
            for p in partners:
                unpack(level, p)

        arrive([(0, 0, -1), (0, 0, 1)])
        for z in (-1, 1):
            plane = 4 + (z > 0)
            sources = [((0, 0, 0), caps[flag(z)]), ((0, 0, z), got[0, 0, z][...])]
            put(plane, ("face", 0), column_of(0, 0, z), area, sources)
            add_plane(plane, faces[plane - 2], ("z", last - near(z)))
        arrive([(0, -1, 0), (0, 1, 0)] + [(0, y, z) for y in (-1, 1) for z in (-1, 1)])
        for y in (-1, 1):
            plane = 2 + (y > 0)
            flat = got[0, y, 0].reshape(edge * edge, slots * c0)
            own = volume[:, line_y(y), :].reshape(edge * edge, slots * c0)
            sources = [((0, 0, 0), own), ((0, y, 0), flat[...])]
            put(plane, ("face", 0), column_of(0, y, 0), area, sources)
            for z in (-1, 1):
                sources = [
                    ((0, 0, 0), lines[flag(z), flag(y)]),
                    ((0, y, 0), flat[skip(near(z)), :]),
                    ((0, 0, z), got[0, 0, z][skip(near(y)), :]),
                    ((0, y, z), got[0, y, z][...]),
                ]
                put(plane, ("column", beyond(z)), column_of(0, y, z), edge, sources)
            add_plane(plane, faces[plane - 2], ("y", (last - near(y)) * edge))
        for x in (-1, 1):
            plane, xe = (x > 0) + 0, near(x)
            put(plane, ("face", 0), column_of(x, 0, 0), area, [((0, 0, 0), volume[xe])])
            for y in (-1, 1):
                sources = [((0, 0, 0), volume[xe, line_y(y), :]), ((0, y, 0), got[0, y, 0][xe])]
                put(plane, ("row", beyond(y)), column_of(x, y, 0), edge, sources)
            for z in (-1, 1):
                span = slice(xe * edge, xe * edge + edge)
                sources = [((0, 0, 0), caps[flag(z), span, :]), ((0, 0, z), got[0, 0, z][span, :])]
                put(plane, ("column", beyond(z)), column_of(x, 0, z), edge, sources)
            for y in (-1, 1):
                for z in (-1, 1):
                    at = xe * edge + near(y)
                    sources = [
                        ((0, 0, 0), lines[flag(z), flag(y), xe : xe + 1, :]),
                        ((0, y, 0), got[0, y, 0][xe, near(z) : near(z) + 1, :]),
                        ((0, 0, z), got[0, 0, z][at : at + 1, :]),
                        ((0, y, z), got[0, y, z][xe : xe + 1, :]),
                    ]
                    put(plane, ("cell", (beyond(y), beyond(z))), column_of(x, y, z), 1, sources)
        add_plane(half, weights[2 * half], ("x", pl.multiple_of(half * last * area, area)))
        arrive([p for p in order_of[::-1] if p[0] == 1])
        plane = 1 - half
        x = 1 - 2 * half
        face = got[1, 0, 0]
        put(plane, ("face", 0), column_of(x, 0, 0), area, [((1, 0, 0), face[0])], True)
        for y in (-1, 1):
            sources = [((1, 0, 0), face[0, line_y(y), :]), ((1, y, 0), got[1, y, 0][0])]
            put(plane, ("row", beyond(y)), column_of(x, y, 0), edge, sources, True)
        for z in (-1, 1):
            sources = [((1, 0, 0), face[0, skip(near(z)), :]), ((1, 0, z), got[1, 0, z][...])]
            put(plane, ("column", beyond(z)), column_of(x, 0, z), edge, sources, True)
        for y in (-1, 1):
            for z in (-1, 1):
                at = near(y) * edge + near(z)
                sources = [
                    ((1, 0, 0), face[0, at : at + 1, :]),
                    ((1, y, 0), got[1, y, 0][0, near(z) : near(z) + 1, :]),
                    ((1, 0, z), got[1, 0, z][near(y) : near(y) + 1, :]),
                    ((1, y, z), got[1, y, z][pl.ds(half * last, 1), :]),
                ]
                put(plane, ("cell", (beyond(y), beyond(z))), column_of(x, y, z), 1, sources, True)
        add_plane(plane, weights[2 * plane], ("x", pl.multiple_of(plane * last * area, area)))

    def surface(level):
        volume, caps, lines = level["v"], level["caps"], level["lines"]
        for k, z in enumerate((0, edge - 1)):
            for x in range(edge):
                caps[k, x * edge : (x + 1) * edge, :] = volume[x, pl.ds(z, edge, stride=edge), :]
            for j, y in enumerate((0, edge - 1)):
                line = caps[k, pl.ds(y, edge, stride=edge), :]
                lines[k, j] = line
                level["send_l"][k, j] = line.astype(BF16)
            level["send_z"][k] = caps[k].astype(BF16)
        for j, y in enumerate((0, edge - 1)):
            face = volume[:, y * edge : (y + 1) * edge, :].reshape(area, slots * c0)
            level["send_y"][j] = face.astype(BF16)

    def fill_faces(weights, target):
        width = slots * c0
        for k in range(2):
            for i in range(3):
                target[k, :, 3 * i * width : 3 * (i + 1) * width] = weights[i, :, 6 * k * width : (6 * k + 3) * width]
                for j in range(3):
                    at, tap = (3 * i + j) * width, (3 * j + 2 * k) * width
                    target[2 + k, :, at : at + width] = weights[i, :, tap : tap + width]

    taps = wc.shape[2] - 1

    pairs = n // 2
    pair, core = m // 2, m % 2
    partner = pair * 2 + 1 - core

    def span(part):
        first, last = (taps + 1) * part // PIECES, (taps + 1) * (part + 1) // PIECES
        return pl.ds(first, last - first)

    def weight_copy(part, r, owner, target):
        return pltpu.make_async_remote_copy(
            src_ref=wc.at[core, owner, span(part)],
            dst_ref=wc.at[core, owner, span(part)],
            send_sem=wsend.at[part, r],
            recv_sem=wrecv.at[part, r],
            device_id=(g, target * 2 + core),
            device_id_type=MESH,
        )

    def share_copy(part, owner_core):
        return pltpu.make_async_remote_copy(
            src_ref=wc.at[owner_core, :, span(part)],
            dst_ref=wc.at[owner_core, :, span(part)],
            send_sem=wsend.at[part, 0],
            recv_sem=wrecv.at[part, 0],
            device_id=(g, partner),
            device_id_type=MESH,
        )

    def send_weights(part):
        for r in range(1, pairs):
            weight_copy(part, r, pair, (pair + r) % pairs).start()

    def hand_on(part):
        for r in range(1, pairs):
            other = (pair + pairs - r) % pairs
            weight_copy(part, r, other, other).wait_recv()
        share_copy(part, core).start()

    def diagonal(matrix):
        empty = jnp.zeros_like(matrix)
        return jnp.concatenate([matrix, empty], axis=1), jnp.concatenate([empty, matrix], axis=1)

    def fill_diagonal(weights, target):
        rows, width = weights.shape[1], 2 * weights.shape[2]
        for t in range(weights.shape[0]):
            top, bottom = diagonal(weights[t])
            at = (t % 9) * width
            target[t // 9, 0:rows, at : at + width] = top
            target[t // 9, rows : 2 * rows, at : at + width] = bottom

    def fill_upright(weights, target):
        rows, width = weights.shape[1:]
        for t in range(weights.shape[0]):
            empty = jnp.zeros((rows, width), BF16)
            for b in range(slots):
                at = (t % 9 * slots + b) * rows
                for other in range(slots):
                    there = weights[t] if other == b else empty
                    target[t // 9, at : at + rows, other * width : (other + 1) * width] = there

    def convolve_own(level, weights):
        lanes = slots * c0
        inside = slice(1, edge + 1)
        ext_leaf[inside, inside, inside, :] = level["v"][...].reshape(edge, edge, edge, lanes)
        for k in range(9):
            y, z = k // 3, k % 3
            rows = ext_leaf[:, y : y + edge, z : z + edge, :].reshape(edge + 2, edge * edge, lanes)
            im_leaf[:, :, k * lanes : (k + 1) * lanes] = rows.astype(BF16)
        total = None
        for x in range(3):
            window = im_leaf[x : x + edge].reshape(edge**3, 9 * lanes)
            term = matmul_nt(window, weights[x])
            total = term if total is None else total + term
        acc[...] = total

    leaf_a, leaf_b, mid, low = levels
    loads[-1].wait()
    packed = feat[...].reshape(slots * c0, voxels).astype(F32)
    turned = packed.T
    leaf_a["v"][...] = turned.reshape(edge, area, slots * c0)
    leaf_a["flat"][...] = turned.astype(BF16)
    surface(leaf_a)
    ext_leaf[...] = jnp.zeros_like(ext_leaf)
    planes[...] = jnp.zeros_like(planes)
    peers = n - 1
    for p in far:
        peers = peers + has(p).astype(jnp.int32)
    pl.semaphore_wait(barrier, peers)

    send(leaf_a)
    loads[4].wait()
    loads[5].wait()
    wc[core, pair, taps] = jnp.concatenate([wp[...]] * (c1 // c0), axis=1)
    send_weights(0)
    loads[0].wait()
    fill_diagonal(w1, b1)
    fill_faces(b1, f1)
    convolve_own(leaf_a, b1)
    loads[6].wait()
    loads[7].wait()
    loads[8].wait()
    fill_gather()
    halo(leaf_a, b1, f1)
    first = rounded_gelu(acc[...])

    leaf_b["flat"][...] = first
    leaf_b["v"][...] = first.astype(F32).reshape(edge, area, slots * c0)
    surface(leaf_b)
    send(leaf_b)
    send_weights(1)
    loads[1].wait()
    fill_diagonal(w2, b2)
    fill_faces(b2, f2)
    convolve_own(leaf_b, b2)
    hand_on(0)
    sent(leaf_a)
    halo(leaf_b, b2, f2)
    second = rounded_gelu(acc[...])

    def halving(length):
        small = length // 2
        row = lax.broadcasted_iota(jnp.int32, (small**3, length**3), 0)
        column = lax.broadcasted_iota(jnp.int32, (small**3, length**3), 1)
        x, y, z = column // (length * length), column // length % length, column % length
        hit = row == (x // 2) * small * small + (y // 2) * small + z // 2
        return jnp.where(hit, 0.125, 0.0).astype(BF16)

    side = edge // 2
    pooled = jnp.dot(halving(edge), second, preferred_element_type=F32).astype(BF16).astype(F32)
    for x in range(side):
        for y in range(side):
            at = (x * side + y) * side
            mid["v"][x, y] = pooled[at : at + side]
    caps_of(mid)
    send(mid)
    send_weights(2)
    loads[2].wait()
    fill_upright(wm, bm)
    hand_on(1)
    sent(leaf_b)
    receive(mid)
    extend(mid)
    lanes = slots * c0
    for k in range(9):
        ty, tz = k // 3, k % 3
        for y in range(side):
            im_mid[:, y * side : (y + 1) * side, k * lanes : (k + 1) * lanes] = mid["ext"][:, y + ty, tz : tz + side, :]
    total = None
    for x in range(3):
        window = im_mid[x : x + side].astype(BF16).reshape(side**3, 9 * lanes)
        term = jnp.dot(window, bm[x], preferred_element_type=F32)
        total = term if total is None else total + term
    middle = rounded_gelu(total)

    pooled = jnp.dot(halving(side), middle, preferred_element_type=F32)
    pooled = jnp.concatenate([pooled[:, b * c1 : (b + 1) * c1] for b in range(slots)], axis=0).astype(BF16)
    low["rows"][...] = pooled
    send(low)
    loads[3].wait()
    skip_top, skip_bottom = diagonal(wo[:, :c0])
    skip_weights = jnp.concatenate([skip_top, skip_bottom], axis=0)
    mixed = matmul_nt(skip_weights, second)
    hand_on(2)
    for part in range(PIECES):
        share_copy(part, 1 - core).wait_recv()
    c2 = n * wc.shape[3]
    rows = slots * cells
    project = lax.dot_general(
        wo[:, c0:], wc[:, :, taps].reshape(c2, c1)[:, :c0], (((1,), (1,)), ((), ())), preferred_element_type=F32
    )
    high = project.astype(BF16)
    project = jnp.concatenate([high, (project - high.astype(F32)).astype(BF16)], axis=0)
    row = lax.broadcasted_iota(jnp.int32, (3 * rows, voxels), 0) % cells
    column = lax.broadcasted_iota(jnp.int32, (3 * rows, voxels), 1)
    factor = edge // small
    x, y, z = column // area, column // edge % edge, column % edge
    widen = jnp.where(row == (x // factor) * small * small + (y // factor) * small + z // factor, 1.0, 0.0).astype(BF16)
    receive(low)
    sources = [pooled]
    for i, p in enumerate(PARTNERS):
        sources.append(jnp.where(has(p), low["got"][i], jnp.zeros_like(pooled)))
    spare = gather.shape[1] - len(sources) * slots * cells
    sources.append(jnp.zeros((spare, c1), BF16))
    spread = jnp.dot(gather[...], jnp.concatenate(sources, axis=0), preferred_element_type=F32).astype(BF16)
    window = jnp.concatenate([spread[t * rows : (t + 1) * rows] for t in range(taps)], axis=1)
    weights = jnp.concatenate([wc[:, :, t].reshape(c2, c1) for t in range(taps)], axis=1)
    hidden = rounded_gelu(matmul_nt(weights, jnp.concatenate([window] * 3, axis=0)))
    lifted = jnp.dot(project, hidden, preferred_element_type=F32)
    lifted = lifted[:c0] + lifted[c0:]
    high = lifted.astype(BF16).astype(F32)
    middle_bits = (lifted - high).astype(BF16).astype(F32)
    low_bits = lifted - high - middle_bits
    column = lax.broadcasted_iota(jnp.int32, lifted.shape, 1)
    terms = jnp.where(column < rows, high, jnp.where(column < 2 * rows, middle_bits, low_bits))
    owner_of = column % rows // cells
    terms = jnp.concatenate([jnp.where(owner_of == b, terms, 0.0) for b in range(slots)], axis=0).astype(BF16)
    mixed = mixed + jnp.dot(terms, widen, preferred_element_type=F32)
    owner = lax.broadcasted_iota(jnp.int32, mixed.shape, 0) // c0
    mixed = jnp.where(owner < live[0], mixed, 0.0).astype(BF16)
    for b in range(slots):
        out[b] = mixed[b * c0 : (b + 1) * c0]

    sent(mid)
    sent(low)
    for part in range(PIECES):
        share_copy(part, core).wait_send()
        for r in range(1, pairs):
            weight_copy(part, r, pair, (pair + r) % pairs).wait_send()


def leaf_scratch(length, lanes):
    def got(partner):
        h, y, z = partner
        if z == 0:
            return pltpu.VMEM((1 if h else length, length if y else length**2, lanes), F32)
        return pltpu.VMEM((length if h or y else length**2, lanes), F32)

    return dict(
        v=pltpu.VMEM((length, length**2, lanes), F32),
        caps=pltpu.VMEM((2, length**2, lanes), F32),
        lines=pltpu.VMEM((2, 2, length, lanes), F32),
        flat=pltpu.VMEM((length**3, lanes), BF16),
        send_y=pltpu.VMEM((2, length**2, lanes), BF16),
        send_z=pltpu.VMEM((2, length**2, lanes), BF16),
        send_l=pltpu.VMEM((2, 2, length, lanes), BF16),
        land=[pltpu.VMEM((length**2 if sum(map(abs, p)) == 1 else length, lanes), BF16) for p in PARTNERS],
        got=[got(p) for p in PARTNERS],
    )


def coarse_table(slots, small):
    cells = small**3
    table = np.zeros((len(OFFSETS) * slots * cells, 128), np.float32)
    row = 0
    for tap in OFFSETS:
        for b in range(slots):
            for cell in np.ndindex(small, small, small):
                there = np.array(cell) + np.array(tap)
                x, y, z = there // small + 1
                table[row, b * 27 + 9 * x + 3 * y + z] = 1
                x, y, z = there % small
                table[row, slots * 27 + (x * small + y) * small + z] = 1
                row += 1
    return jnp.asarray(table, BF16)


def level_scratch(length, lanes):
    def got(partner):
        h, y, z = partner
        return pltpu.VMEM((1 if h else length, 1 if y else length, 1 if z else length, lanes), F32)

    return dict(
        v=pltpu.VMEM((length, length, length, lanes), F32),
        caps=pltpu.VMEM((2, length, length, 1, lanes), F32),
        ext=pltpu.VMEM((length + 2,) * 3 + (lanes,), F32),
        got=[got(p) for p in PARTNERS],
    )


def shards(grps, n, features, live_counts, neighbours, w_first, w_second, w_middle, w_coarse, w_project, w_output):
    slots, c0, voxels = features.shape
    edge = round(voxels ** (1 / 3))
    w_middle = jnp.swapaxes(w_middle, 1, 2)
    taps, _, c1 = w_middle.shape
    lanes = slots * c0
    side, small = edge // 2, edge // 4
    levels = [
        leaf_scratch(edge, lanes),
        leaf_scratch(edge, lanes),
        level_scratch(side, lanes),
        dict(
            rows=pltpu.VMEM((slots * small**3, c1), BF16),
            got=pltpu.VMEM((len(PARTNERS), slots * small**3, c1), BF16),
        ),
    ]
    table = coarse_table(slots, small)
    mats = [
        pltpu.VMEM(features.shape, BF16),
        pltpu.VMEM(w_first.shape, BF16),
        pltpu.VMEM(w_second.shape, BF16),
        pltpu.VMEM(w_middle.shape, BF16),
        pltpu.VMEM(w_output.shape, BF16),
        pltpu.VMEM((2, n // 2, taps + 1) + w_coarse.shape[1:], BF16),
        pltpu.VMEM(w_project.shape, BF16),
        pltpu.VMEM((3, lanes, 9 * lanes), BF16),
        pltpu.VMEM((3, lanes, 9 * lanes), BF16),
        pltpu.VMEM((4, lanes, 9 * lanes), BF16),
        pltpu.VMEM((4, lanes, 9 * lanes), BF16),
        pltpu.VMEM((3, 9 * lanes, slots * c1), BF16),
        pltpu.VMEM((edge + 2, edge * edge, 9 * lanes), BF16),
        pltpu.VMEM((side + 2, side * side, 9 * lanes), F32),
        pltpu.VMEM(table.shape, BF16),
        pltpu.VMEM((table.shape[0], 3 * 128), BF16),
        pltpu.VMEM((edge + 2,) * 3 + (lanes,), F32),
        pltpu.VMEM((6, (edge + 2) * 2 * edge, lanes), F32),
        pltpu.VMEM((edge**3, lanes), F32),
    ]
    sems = [
        pltpu.SemaphoreType.DMA((10,)),
        pltpu.SemaphoreType.DMA((PIECES, n // 2)),
        pltpu.SemaphoreType.DMA((PIECES, n // 2)),
        pltpu.SemaphoreType.DMA((2, len(PARTNERS))),
        pltpu.SemaphoreType.DMA((2, len(PARTNERS))),
    ]
    smem = pl.BlockSpec(memory_space=pltpu.SMEM)
    vmem = pl.BlockSpec(memory_space=pltpu.VMEM)
    stay = pl.BlockSpec(memory_space=pl.ANY)
    return pl.pallas_call(
        functools.partial(kernel, grps, n),
        out_shape=pltpu.VMEM(features.shape, BF16),
        in_specs=[stay] * 10,
        out_specs=vmem,
        scratch_shapes=[levels, mats, pltpu.SMEM(live_counts.shape, jnp.int32), pltpu.SMEM(neighbours.shape, jnp.int32), sems],
        compiler_params=pltpu.CompilerParams(collective_id=0, has_side_effects=True),
    )(features, live_counts, neighbours, w_first, w_second, w_middle, w_coarse, w_project, w_output, table)


def solution(mesh):
    in_specs = (
        P(("grp", "ch"), None, None),
        P(("grp", "ch")),
        P(("grp", "ch"), None),
        P(),
        P(),
        P(),
        P(None, "ch", None),
        P("ch", None),
        P(),
    )
    return jax.shard_map(
        functools.partial(shards, mesh.shape["grp"], mesh.shape["ch"]),
        mesh=mesh,
        in_specs=in_specs,
        out_specs=P(("grp", "ch"), None, None),
        check_vma=False,
    )
```

```python
import functools

import numpy as np

import jax
import jax.numpy as jnp
from jax import lax
from jax.experimental import pallas as pl
from jax.experimental.pallas import tpu as pltpu
from jax.sharding import PartitionSpec as P

MESH = pl.DeviceIdType.MESH
F32, BF16 = jnp.float32, jnp.bfloat16
STEPS = (-1, 0, 1)
OFFSETS = [(x, y, z) for x in STEPS for y in STEPS for z in STEPS]
PARTNERS = [(h, y, z) for h in (0, 1) for y in STEPS for z in STEPS if (h, y, z) != (0, 0, 0)]
PIECES = 3


def matmul_nt(left, right):
    return lax.dot_general(left, right, (((1,), (1,)), ((), ())), preferred_element_type=F32)


def rounded_gelu(value):
    scale = (2 / np.pi) ** 0.5
    half = 0.5 * value
    return (half + half * jnp.tanh(value * (scale + scale * 0.044715 * (value * value)))).astype(BF16)


def kernel(grps, n, feat_any, live_any, neigh_any, w1_any, w2_any, wm_any, wc_any, wp_any, wo_any, table_any, out, levels, mats, live, neigh, sems):
    g, m = lax.axis_index("grp"), lax.axis_index("ch")
    q = n // 2
    half, place_y = m // q, m % q
    slots, c0, voxels = feat_any.shape
    edge = round(voxels ** (1 / 3))
    c1 = wm_any.shape[2]

    def has(partner):
        _, y, z = partner
        return (place_y + y >= 0) & (place_y + y < q) & (g + z >= 0) & (g + z < grps)

    def coords(partner):
        h, y, z = partner
        return g + z, ((1 - half) if h else half) * q + place_y + y

    barrier = pltpu.get_barrier_semaphore()
    far = [p for p in PARTNERS if p[2] != 0]
    for p in sorted(far, key=lambda p: -sum(abs(s) for s in p)):

        @pl.when(has(p))
        def _():
            pl.semaphore_signal(barrier, inc=1, device_id=coords(p), device_id_type=MESH)

    for r in range(1, n):
        pl.semaphore_signal(barrier, inc=1, device_id=(g, (m + r) % n), device_id_type=MESH)

    (feat, w1, w2, wm, wo, wc, wp, b1, b2, f1, f2, bm, im_leaf, im_mid, table, gather, ext_leaf, planes, acc) = mats
    (local_sem, wsend, wrecv, hsend, hrecv) = sems
    for i, level in enumerate(levels):
        level.update(send=hsend, recv=hrecv.at[i % 2])
    loads = [
        pltpu.make_async_copy(source, target, local_sem.at[i])
        for i, (source, target) in enumerate(
            [(w1_any, w1), (w2_any, w2), (wm_any, wm), (wo_any, wo), (wc_any, wc.at[m % 2, m // 2, pl.ds(0, wc_any.shape[0])]), (wp_any, wp), (live_any, live), (neigh_any, neigh), (table_any, table), (feat_any, feat)]
        )
    ]
    for load in loads[-1:] + loads[:-1]:
        load.start()

    area = edge * edge

    def leaf_piece(level, partner):
        h, y, z = partner
        upper, right = (1 if z > 0 else 0), (1 if y > 0 else 0)
        far_side = 1 - half
        if z:
            if y:
                return level["send_l"].at[upper, right]
            if h:
                return level["send_z"].at[upper, pl.ds(pl.multiple_of(far_side * (area - edge), edge), edge)]
            return level["send_z"].at[upper]
        if not h:
            return level["send_y"].at[right]
        start, size = far_side * (edge - 1) * area + right * (area - edge if y else 0), edge if y else area
        return level["flat"].at[pl.ds(pl.multiple_of(start, edge), size)]

    def unpack(level, partner):
        index = PARTNERS.index(partner)
        value = level["land"][index][...].astype(F32)
        target = level["got"][index]
        target[...] = value.reshape(target.shape)

    def piece_of(level, partner):
        if "lines" in level:
            return leaf_piece(level, partner)
        if "rows" in level:
            return level["rows"]
        h, y, z = partner
        volume, caps = level["v"], level["caps"]
        length = volume.shape[0]
        pick_x = pl.ds((1 - half) * (length - 1), 1) if h else slice(None)
        pick_y = slice(None) if y == 0 else (pl.ds(length - 1, 1) if y > 0 else pl.ds(0, 1))
        if z == 0:
            return volume.at[pick_x, pick_y]
        return caps.at[1 if z > 0 else 0, pick_x, pick_y]

    def copy_to(level, index):
        h, y, z = PARTNERS[index]
        back = PARTNERS.index((h, -y, -z))
        return pltpu.make_async_remote_copy(
            src_ref=piece_of(level, PARTNERS[index]),
            dst_ref=level["got"].at[back] if "rows" in level else level.get("land", level["got"])[back],
            send_sem=level["send"].at[index],
            recv_sem=level["recv"].at[back],
            device_id=coords(PARTNERS[index]),
            device_id_type=MESH,
        )

    order = sorted(range(len(PARTNERS)), key=lambda i: -sum(abs(s) for s in PARTNERS[i]))

    def caps_of(level):
        volume, caps = level["v"], level["caps"]
        length = volume.shape[0]
        caps[0] = volume[:, :, 0:1, :]
        caps[1] = volume[:, :, length - 1 : length, :]

    def send(level):
        for i in order:

            @pl.when(has(PARTNERS[i]))
            def _():
                copy_to(level, i).start()

    order_of = [PARTNERS[i] for i in order]

    def sent(level):
        for i in order:

            @pl.when(has(PARTNERS[i]))
            def _():
                copy_to(level, i).wait_send()

    def wait_for(level, partners):
        for h, y, z in partners:

            @pl.when(has((h, -y, -z)))
            def _():
                copy_to(level, PARTNERS.index((h, y, z))).wait_recv()

    def receive(level):
        for i in order:
            h, y, z = PARTNERS[i]

            @pl.when(has((h, -y, -z)))
            def _():
                copy_to(level, i).wait_recv()

    def extend(level, own):
        volume, ext, caps = level["v"], level["ext"], level["caps"]
        length, lanes = volume.shape[0], volume.shape[3]
        middle = lanes // 2
        lane = lax.broadcasted_iota(jnp.int32, (1, 1, 1, lanes), 3)
        upper = (lane >= middle).astype(jnp.int32)
        if own:
            ext[1 : length + 1, 1 : length + 1, 1 : length + 1, :] = volume[...]
        firsts = {}
        for p in [(0, 0, 0)] + PARTNERS:
            a, b = coords(p)
            firsts[p] = jnp.where(has(p), (a * n + b) * 2, -8)

        def source_at(step):
            return slice(0, length) if step == 0 else (slice(0, 1) if step > 0 else slice(length - 1, length))

        def target_at(step):
            return slice(1, length + 1) if step == 0 else (slice(0, 1) if step < 0 else slice(length + 1, length + 2))

        for column, (x, y, z) in enumerate(OFFSETS):
            if (x, y, z) == (0, 0, 0):
                continue
            wanted = jnp.where(upper == 1, neigh[1, column], neigh[0, column])
            shape = tuple(length if s == 0 else 1 for s in (x, y, z)) + (lanes,)
            wanted = jnp.broadcast_to(wanted, shape)
            upper_full = jnp.broadcast_to(upper, shape)
            target = (target_at(x), target_at(y), target_at(z))
            value = jnp.zeros(shape, F32) if own else ext[target]
            for h in (0, 1) if x else (0,):
                for cy in (0, y) if y else (0,):
                    for cz in (0, z) if z else (0,):
                        p = (h, cy, cz)
                        if (p == (0, 0, 0)) != own:
                            continue
                        at_x = slice(0, 1) if h else source_at(x)
                        at_y = slice(0, 1) if cy else source_at(y)
                        at_z = slice(0, 1) if cz else source_at(z)
                        if p == (0, 0, 0):
                            if z:
                                found = caps[0 if z > 0 else 1, at_x, at_y, :, :]
                            else:
                                found = volume[at_x, at_y, at_z, :]
                        else:
                            found = level["got"][PARTNERS.index(p)][at_x, at_y, at_z, :]
                        swapped = jnp.concatenate([found[..., middle:], found[..., :middle]], axis=3)
                        value = jnp.where(
                            wanted == firsts[p] + upper_full,
                            found,
                            jnp.where(wanted == firsts[p] + 1 - upper_full, swapped, value),
                        )
            ext[target] = value

    half_lanes = slots * c0 // 2
    lane = lax.broadcasted_iota(jnp.int32, (edge, slots * c0), 1)
    block_of = (lane >= half_lanes).astype(jnp.int32)
    first_of = {}
    for p in [(0, 0, 0)] + PARTNERS:
        a, b = coords(p)
        first_of[p] = jnp.where(has(p), (a * n + b) * 2, -8)

    def choose(column, rows, sources, value=None):
        wanted = jnp.where(block_of == 1, neigh[1, column], neigh[0, column])
        owner = block_of
        if rows < edge:
            wanted, owner = wanted[:rows], owner[:rows]
        for p, found in sources:
            pieces = [found[r : r + min(rows, edge)] for r in range(0, rows, edge)]
            straight, crossed = wanted == first_of[p] + owner, wanted == first_of[p] + 1 - owner
            old = value if value is not None else [jnp.zeros_like(piece) for piece in pieces]
            value = [
                jnp.where(straight, piece, jnp.where(crossed, pltpu.roll(piece, half_lanes, 1), before))
                for piece, before in zip(pieces, old)
            ]
        return value

    def spots(plane, kind):
        axis, place = kind
        pitch = 2 * edge
        if axis == "face":
            return [(plane, slice((r + 1) * pitch + 1, (r + 1) * pitch + 1 + edge)) for r in range(edge)]
        if axis == "row":
            return [(plane, slice(place * pitch + 1, place * pitch + 1 + edge))]
        if axis == "column":
            return [(plane, pl.ds(pitch + place, edge, stride=pitch))]
        return [(plane, slice(place[0] * pitch + place[1], place[0] * pitch + place[1] + 1))]

    def put(plane, kind, column, rows, sources, add=False):
        where = spots(plane, kind)
        value = choose(column, rows, sources, [planes[spot] for spot in where] if add else None)
        for spot, part in zip(where, value):
            planes[spot] = part

    def add_plane(plane, weights, where):
        parts = []
        for i in range(3):
            for j in range(3):
                rows = [planes[plane, (r + i) * 2 * edge + j : (r + i) * 2 * edge + j + edge, :] for r in range(edge)]
                parts.append(jnp.concatenate(rows, axis=0).astype(BF16))
        update = matmul_nt(jnp.concatenate(parts, axis=1), weights)
        axis, at = where
        if axis == "x":
            acc[pl.ds(at, area), :] += update
            return
        for r in range(edge):
            rows = update[r * edge : (r + 1) * edge]
            if axis == "y":
                acc[r * area + at : r * area + at + edge, :] += rows
            else:
                acc[pl.ds(r * area + at, edge, stride=edge), :] += rows

    small = edge // 4
    cells = small**3

    def fill_gather():
        sub = lax.broadcasted_iota(jnp.int32, (8, gather.shape[1] // 3), 0)
        col = lax.broadcasted_iota(jnp.int32, (8, gather.shape[1] // 3), 1)
        width = sub.shape[1]
        entries = [neigh[b, d] * cells for b in range(slots) for d in range(27)] + list(range(cells))
        blocks = []
        for start in range(0, width, 8):
            block = jnp.zeros(sub.shape, jnp.int32)
            for s, entry in enumerate(entries[start : start + 8]):
                block = jnp.where(sub == s, entry, block)
            blocks.append(block.astype(F32))
        keys = jnp.dot(table[...], jnp.concatenate(blocks, axis=0).astype(BF16), preferred_element_type=F32)
        rows = slots * cells
        for k in range(3):
            offer = jnp.full(sub.shape, -1000, jnp.int32)
            for i, p in enumerate([(0, 0, 0)] + PARTNERS):
                at = i * rows - k * width
                offer = jnp.where((col >= at) & (col < at + rows), first_of[p] * cells + col - at, offer)
            offer = jnp.broadcast_to(offer[:1].astype(F32), keys.shape)
            gather[:, k * width : (k + 1) * width] = jnp.where(keys == offer, 1.0, 0.0).astype(BF16)

    def column_of(x, y, z):
        return 9 * (x + 1) + 3 * (y + 1) + z + 1

    def halo(level, weights, faces):
        volume, caps, lines = level["v"], level["caps"], level["lines"]
        got = {p: level["got"][i] for i, p in enumerate(PARTNERS)}
        last = edge - 1
        near = lambda s: 0 if s > 0 else last
        beyond = lambda s: 0 if s < 0 else edge + 1
        flag = lambda s: 0 if s > 0 else 1
        line_y = lambda y: slice(near(y) * edge, near(y) * edge + edge)
        skip = lambda start: pl.ds(start, edge, stride=edge)

        def arrive(partners):
            wait_for(level, partners)
            for p in partners:
                unpack(level, p)

        arrive([(0, 0, -1), (0, 0, 1)])
        for z in (-1, 1):
            plane = 4 + (z > 0)
            sources = [((0, 0, 0), caps[flag(z)]), ((0, 0, z), got[0, 0, z][...])]
            put(plane, ("face", 0), column_of(0, 0, z), area, sources)
            add_plane(plane, faces[plane - 2], ("z", last - near(z)))
        arrive([(0, -1, 0), (0, 1, 0)] + [(0, y, z) for y in (-1, 1) for z in (-1, 1)])
        for y in (-1, 1):
            plane = 2 + (y > 0)
            flat = got[0, y, 0].reshape(edge * edge, slots * c0)
            own = volume[:, line_y(y), :].reshape(edge * edge, slots * c0)
            sources = [((0, 0, 0), own), ((0, y, 0), flat[...])]
            put(plane, ("face", 0), column_of(0, y, 0), area, sources)
            for z in (-1, 1):
                sources = [
                    ((0, 0, 0), lines[flag(z), flag(y)]),
                    ((0, y, 0), flat[skip(near(z)), :]),
                    ((0, 0, z), got[0, 0, z][skip(near(y)), :]),
                    ((0, y, z), got[0, y, z][...]),
                ]
                put(plane, ("column", beyond(z)), column_of(0, y, z), edge, sources)
            add_plane(plane, faces[plane - 2], ("y", (last - near(y)) * edge))
        for x in (-1, 1):
            plane, xe = (x > 0) + 0, near(x)
            put(plane, ("face", 0), column_of(x, 0, 0), area, [((0, 0, 0), volume[xe])])
            for y in (-1, 1):
                sources = [((0, 0, 0), volume[xe, line_y(y), :]), ((0, y, 0), got[0, y, 0][xe])]
                put(plane, ("row", beyond(y)), column_of(x, y, 0), edge, sources)
            for z in (-1, 1):
                span = slice(xe * edge, xe * edge + edge)
                sources = [((0, 0, 0), caps[flag(z), span, :]), ((0, 0, z), got[0, 0, z][span, :])]
                put(plane, ("column", beyond(z)), column_of(x, 0, z), edge, sources)
            for y in (-1, 1):
                for z in (-1, 1):
                    at = xe * edge + near(y)
                    sources = [
                        ((0, 0, 0), lines[flag(z), flag(y), xe : xe + 1, :]),
                        ((0, y, 0), got[0, y, 0][xe, near(z) : near(z) + 1, :]),
                        ((0, 0, z), got[0, 0, z][at : at + 1, :]),
                        ((0, y, z), got[0, y, z][xe : xe + 1, :]),
                    ]
                    put(plane, ("cell", (beyond(y), beyond(z))), column_of(x, y, z), 1, sources)
        add_plane(half, weights[2 * half], ("x", pl.multiple_of(half * last * area, area)))
        arrive([p for p in order_of[::-1] if p[0] == 1])
        plane = 1 - half
        x = 1 - 2 * half
        face = got[1, 0, 0]
        put(plane, ("face", 0), column_of(x, 0, 0), area, [((1, 0, 0), face[0])], True)
        for y in (-1, 1):
            sources = [((1, 0, 0), face[0, line_y(y), :]), ((1, y, 0), got[1, y, 0][0])]
            put(plane, ("row", beyond(y)), column_of(x, y, 0), edge, sources, True)
        for z in (-1, 1):
            sources = [((1, 0, 0), face[0, skip(near(z)), :]), ((1, 0, z), got[1, 0, z][...])]
            put(plane, ("column", beyond(z)), column_of(x, 0, z), edge, sources, True)
        for y in (-1, 1):
            for z in (-1, 1):
                at = near(y) * edge + near(z)
                sources = [
                    ((1, 0, 0), face[0, at : at + 1, :]),
                    ((1, y, 0), got[1, y, 0][0, near(z) : near(z) + 1, :]),
                    ((1, 0, z), got[1, 0, z][near(y) : near(y) + 1, :]),
                    ((1, y, z), got[1, y, z][pl.ds(half * last, 1), :]),
                ]
                put(plane, ("cell", (beyond(y), beyond(z))), column_of(x, y, z), 1, sources, True)
        add_plane(plane, weights[2 * plane], ("x", pl.multiple_of(plane * last * area, area)))

    def surface(level):
        volume, caps, lines = level["v"], level["caps"], level["lines"]
        for k, z in enumerate((0, edge - 1)):
            for x in range(edge):
                caps[k, x * edge : (x + 1) * edge, :] = volume[x, pl.ds(z, edge, stride=edge), :]
            for j, y in enumerate((0, edge - 1)):
                line = caps[k, pl.ds(y, edge, stride=edge), :]
                lines[k, j] = line
                level["send_l"][k, j] = line.astype(BF16)
            level["send_z"][k] = caps[k].astype(BF16)
        for j, y in enumerate((0, edge - 1)):
            face = volume[:, y * edge : (y + 1) * edge, :].reshape(area, slots * c0)
            level["send_y"][j] = face.astype(BF16)

    def fill_faces(weights, target):
        width = slots * c0
        for k in range(2):
            for i in range(3):
                target[k, :, 3 * i * width : 3 * (i + 1) * width] = weights[i, :, 6 * k * width : (6 * k + 3) * width]
                for j in range(3):
                    at, tap = (3 * i + j) * width, (3 * j + 2 * k) * width
                    target[2 + k, :, at : at + width] = weights[i, :, tap : tap + width]

    taps = wc.shape[2] - 1

    pairs = n // 2
    pair, core = m // 2, m % 2
    partner = pair * 2 + 1 - core

    def span(part):
        first, last = (taps + 1) * part // PIECES, (taps + 1) * (part + 1) // PIECES
        return pl.ds(first, last - first)

    def weight_copy(part, r, owner, target):
        return pltpu.make_async_remote_copy(
            src_ref=wc.at[core, owner, span(part)],
            dst_ref=wc.at[core, owner, span(part)],
            send_sem=wsend.at[part, r],
            recv_sem=wrecv.at[part, r],
            device_id=(g, target * 2 + core),
            device_id_type=MESH,
        )

    def share_copy(part, owner_core):
        return pltpu.make_async_remote_copy(
            src_ref=wc.at[owner_core, :, span(part)],
            dst_ref=wc.at[owner_core, :, span(part)],
            send_sem=wsend.at[part, 0],
            recv_sem=wrecv.at[part, 0],
            device_id=(g, partner),
            device_id_type=MESH,
        )

    def send_weights(part):
        for r in range(1, pairs):
            weight_copy(part, r, pair, (pair + r) % pairs).start()

    def hand_on(part):
        for r in range(1, pairs):
            other = (pair + pairs - r) % pairs
            weight_copy(part, r, other, other).wait_recv()
        share_copy(part, core).start()

    def diagonal(matrix):
        empty = jnp.zeros_like(matrix)
        return jnp.concatenate([matrix, empty], axis=1), jnp.concatenate([empty, matrix], axis=1)

    def fill_diagonal(weights, target):
        rows, width = weights.shape[1], 2 * weights.shape[2]
        for t in range(weights.shape[0]):
            top, bottom = diagonal(weights[t])
            at = (t % 9) * width
            target[t // 9, 0:rows, at : at + width] = top
            target[t // 9, rows : 2 * rows, at : at + width] = bottom

    def fill_upright(weights, target):
        rows, width = weights.shape[1:]
        for t in range(weights.shape[0]):
            empty = jnp.zeros((rows, width), BF16)
            for b in range(slots):
                at = (t % 9 * slots + b) * rows
                for other in range(slots):
                    there = weights[t] if other == b else empty
                    target[t // 9, at : at + rows, other * width : (other + 1) * width] = there

    def convolve_own(level, weights):
        lanes = slots * c0
        inside = slice(1, edge + 1)
        ext_leaf[inside, inside, inside, :] = level["v"][...].reshape(edge, edge, edge, lanes)
        for k in range(9):
            y, z = k // 3, k % 3
            rows = ext_leaf[:, y : y + edge, z : z + edge, :].reshape(edge + 2, edge * edge, lanes)
            im_leaf[:, :, k * lanes : (k + 1) * lanes] = rows.astype(BF16)
        total = None
        for x in range(3):
            window = im_leaf[x : x + edge].reshape(edge**3, 9 * lanes)
            term = matmul_nt(window, weights[x])
            total = term if total is None else total + term
        acc[...] = total

    leaf_a, leaf_b, mid, low = levels
    loads[-1].wait()
    packed = feat[...].reshape(slots * c0, voxels).astype(F32)
    turned = packed.T
    leaf_a["v"][...] = turned.reshape(edge, area, slots * c0)
    leaf_a["flat"][...] = turned.astype(BF16)
    surface(leaf_a)
    ext_leaf[...] = jnp.zeros_like(ext_leaf)
    planes[...] = jnp.zeros_like(planes)
    peers = n - 1
    for p in far:
        peers = peers + has(p).astype(jnp.int32)
    pl.semaphore_wait(barrier, peers)

    send(leaf_a)
    loads[4].wait()
    loads[5].wait()
    wc[core, pair, taps] = jnp.concatenate([wp[...]] * (c1 // c0), axis=1)
    send_weights(0)
    loads[0].wait()
    fill_diagonal(w1, b1)
    fill_faces(b1, f1)
    convolve_own(leaf_a, b1)
    loads[6].wait()
    loads[7].wait()
    loads[8].wait()
    fill_gather()
    sent(leaf_a)
    halo(leaf_a, b1, f1)
    first = rounded_gelu(acc[...])

    leaf_b["flat"][...] = first
    leaf_b["v"][...] = first.astype(F32).reshape(edge, area, slots * c0)
    surface(leaf_b)
    send(leaf_b)
    send_weights(1)
    loads[1].wait()
    fill_diagonal(w2, b2)
    fill_faces(b2, f2)
    convolve_own(leaf_b, b2)
    hand_on(0)
    sent(leaf_b)
    halo(leaf_b, b2, f2)
    second = rounded_gelu(acc[...])

    def halving(length):
        small = length // 2
        row = lax.broadcasted_iota(jnp.int32, (small**3, length**3), 0)
        column = lax.broadcasted_iota(jnp.int32, (small**3, length**3), 1)
        x, y, z = column // (length * length), column // length % length, column % length
        hit = row == (x // 2) * small * small + (y // 2) * small + z // 2
        return jnp.where(hit, 0.125, 0.0).astype(BF16)

    side = edge // 2
    pooled = jnp.dot(halving(edge), second, preferred_element_type=F32).astype(BF16).astype(F32)
    for x in range(side):
        for y in range(side):
            at = (x * side + y) * side
            mid["v"][x, y] = pooled[at : at + side]
    caps_of(mid)
    send(mid)
    send_weights(2)
    loads[2].wait()
    fill_upright(wm, bm)
    extend(mid, True)
    hand_on(1)
    sent(mid)
    receive(mid)
    extend(mid, False)
    lanes = slots * c0
    for k in range(9):
        ty, tz = k // 3, k % 3
        for y in range(side):
            im_mid[:, y * side : (y + 1) * side, k * lanes : (k + 1) * lanes] = mid["ext"][:, y + ty, tz : tz + side, :]
    total = None
    for x in range(3):
        window = im_mid[x : x + side].astype(BF16).reshape(side**3, 9 * lanes)
        term = jnp.dot(window, bm[x], preferred_element_type=F32)
        total = term if total is None else total + term
    middle = rounded_gelu(total)

    pooled = jnp.dot(halving(side), middle, preferred_element_type=F32)
    pooled = jnp.concatenate([pooled[:, b * c1 : (b + 1) * c1] for b in range(slots)], axis=0).astype(BF16)
    low["rows"][...] = pooled
    send(low)
    loads[3].wait()
    skip_top, skip_bottom = diagonal(wo[:, :c0])
    skip_weights = jnp.concatenate([skip_top, skip_bottom], axis=0)
    mixed = matmul_nt(skip_weights, second)
    hand_on(2)
    for part in range(PIECES):
        share_copy(part, 1 - core).wait_recv()
    c2 = n * wc.shape[3]
    rows = slots * cells
    project = lax.dot_general(
        wo[:, c0:], wc[:, :, taps].reshape(c2, c1)[:, :c0], (((1,), (1,)), ((), ())), preferred_element_type=F32
    )
    high = project.astype(BF16)
    project = jnp.concatenate([high, (project - high.astype(F32)).astype(BF16)], axis=0)
    row = lax.broadcasted_iota(jnp.int32, (3 * rows, voxels), 0) % cells
    column = lax.broadcasted_iota(jnp.int32, (3 * rows, voxels), 1)
    factor = edge // small
    x, y, z = column // area, column // edge % edge, column % edge
    widen = jnp.where(row == (x // factor) * small * small + (y // factor) * small + z // factor, 1.0, 0.0).astype(BF16)
    receive(low)
    sources = [pooled]
    for i, p in enumerate(PARTNERS):
        sources.append(jnp.where(has(p), low["got"][i], jnp.zeros_like(pooled)))
    spare = gather.shape[1] - len(sources) * slots * cells
    sources.append(jnp.zeros((spare, c1), BF16))
    spread = jnp.dot(gather[...], jnp.concatenate(sources, axis=0), preferred_element_type=F32).astype(BF16)
    window = jnp.concatenate([spread[t * rows : (t + 1) * rows] for t in range(taps)], axis=1)
    weights = jnp.concatenate([wc[:, :, t].reshape(c2, c1) for t in range(taps)], axis=1)
    hidden = rounded_gelu(matmul_nt(weights, jnp.concatenate([window] * 3, axis=0)))
    lifted = jnp.dot(project, hidden, preferred_element_type=F32)
    lifted = lifted[:c0] + lifted[c0:]
    high = lifted.astype(BF16).astype(F32)
    middle_bits = (lifted - high).astype(BF16).astype(F32)
    low_bits = lifted - high - middle_bits
    column = lax.broadcasted_iota(jnp.int32, lifted.shape, 1)
    terms = jnp.where(column < rows, high, jnp.where(column < 2 * rows, middle_bits, low_bits))
    owner_of = column % rows // cells
    terms = jnp.concatenate([jnp.where(owner_of == b, terms, 0.0) for b in range(slots)], axis=0).astype(BF16)
    mixed = mixed + jnp.dot(terms, widen, preferred_element_type=F32)
    owner = lax.broadcasted_iota(jnp.int32, mixed.shape, 0) // c0
    mixed = jnp.where(owner < live[0], mixed, 0.0).astype(BF16)
    for b in range(slots):
        out[b] = mixed[b * c0 : (b + 1) * c0]

    sent(low)
    for part in range(PIECES):
        share_copy(part, core).wait_send()
        for r in range(1, pairs):
            weight_copy(part, r, pair, (pair + r) % pairs).wait_send()


def leaf_scratch(length, lanes):
    def got(partner):
        h, y, z = partner
        if z == 0:
            return pltpu.VMEM((1 if h else length, length if y else length**2, lanes), F32)
        return pltpu.VMEM((length if h or y else length**2, lanes), F32)

    return dict(
        v=pltpu.VMEM((length, length**2, lanes), F32),
        caps=pltpu.VMEM((2, length**2, lanes), F32),
        lines=pltpu.VMEM((2, 2, length, lanes), F32),
        flat=pltpu.VMEM((length**3, lanes), BF16),
        send_y=pltpu.VMEM((2, length**2, lanes), BF16),
        send_z=pltpu.VMEM((2, length**2, lanes), BF16),
        send_l=pltpu.VMEM((2, 2, length, lanes), BF16),
        land=[pltpu.VMEM((length**2 if sum(map(abs, p)) == 1 else length, lanes), BF16) for p in PARTNERS],
        got=[got(p) for p in PARTNERS],
    )


def coarse_table(slots, small):
    cells = small**3
    table = np.zeros((len(OFFSETS) * slots * cells, 128), np.float32)
    row = 0
    for tap in OFFSETS:
        for b in range(slots):
            for cell in np.ndindex(small, small, small):
                there = np.array(cell) + np.array(tap)
                x, y, z = there // small + 1
                table[row, b * 27 + 9 * x + 3 * y + z] = 1
                x, y, z = there % small
                table[row, slots * 27 + (x * small + y) * small + z] = 1
                row += 1
    return jnp.asarray(table, BF16)


def level_scratch(length, lanes):
    def got(partner):
        h, y, z = partner
        return pltpu.VMEM((1 if h else length, 1 if y else length, 1 if z else length, lanes), F32)

    return dict(
        v=pltpu.VMEM((length, length, length, lanes), F32),
        caps=pltpu.VMEM((2, length, length, 1, lanes), F32),
        ext=pltpu.VMEM((length + 2,) * 3 + (lanes,), F32),
        got=[got(p) for p in PARTNERS],
    )


def shards(grps, n, features, live_counts, neighbours, w_first, w_second, w_middle, w_coarse, w_project, w_output):
    slots, c0, voxels = features.shape
    edge = round(voxels ** (1 / 3))
    w_middle = jnp.swapaxes(w_middle, 1, 2)
    taps, _, c1 = w_middle.shape
    lanes = slots * c0
    side, small = edge // 2, edge // 4
    levels = [
        leaf_scratch(edge, lanes),
        leaf_scratch(edge, lanes),
        level_scratch(side, lanes),
        dict(
            rows=pltpu.VMEM((slots * small**3, c1), BF16),
            got=pltpu.VMEM((len(PARTNERS), slots * small**3, c1), BF16),
        ),
    ]
    table = coarse_table(slots, small)
    mats = [
        pltpu.VMEM(features.shape, BF16),
        pltpu.VMEM(w_first.shape, BF16),
        pltpu.VMEM(w_second.shape, BF16),
        pltpu.VMEM(w_middle.shape, BF16),
        pltpu.VMEM(w_output.shape, BF16),
        pltpu.VMEM((2, n // 2, taps + 1) + w_coarse.shape[1:], BF16),
        pltpu.VMEM(w_project.shape, BF16),
        pltpu.VMEM((3, lanes, 9 * lanes), BF16),
        pltpu.VMEM((3, lanes, 9 * lanes), BF16),
        pltpu.VMEM((4, lanes, 9 * lanes), BF16),
        pltpu.VMEM((4, lanes, 9 * lanes), BF16),
        pltpu.VMEM((3, 9 * lanes, slots * c1), BF16),
        pltpu.VMEM((edge + 2, edge * edge, 9 * lanes), BF16),
        pltpu.VMEM((side + 2, side * side, 9 * lanes), F32),
        pltpu.VMEM(table.shape, BF16),
        pltpu.VMEM((table.shape[0], 3 * 128), BF16),
        pltpu.VMEM((edge + 2,) * 3 + (lanes,), F32),
        pltpu.VMEM((6, (edge + 2) * 2 * edge, lanes), F32),
        pltpu.VMEM((edge**3, lanes), F32),
    ]
    sems = [
        pltpu.SemaphoreType.DMA((10,)),
        pltpu.SemaphoreType.DMA((PIECES, n // 2)),
        pltpu.SemaphoreType.DMA((PIECES, n // 2)),
        pltpu.SemaphoreType.DMA((len(PARTNERS),)),
        pltpu.SemaphoreType.DMA((2, len(PARTNERS))),
    ]
    smem = pl.BlockSpec(memory_space=pltpu.SMEM)
    vmem = pl.BlockSpec(memory_space=pltpu.VMEM)
    stay = pl.BlockSpec(memory_space=pl.ANY)
    return pl.pallas_call(
        functools.partial(kernel, grps, n),
        out_shape=pltpu.VMEM(features.shape, BF16),
        in_specs=[stay] * 10,
        out_specs=vmem,
        scratch_shapes=[levels, mats, pltpu.SMEM(live_counts.shape, jnp.int32), pltpu.SMEM(neighbours.shape, jnp.int32), sems],
        compiler_params=pltpu.CompilerParams(collective_id=0, has_side_effects=True),
    )(features, live_counts, neighbours, w_first, w_second, w_middle, w_coarse, w_project, w_output, table)


def solution(mesh):
    in_specs = (
        P(("grp", "ch"), None, None),
        P(("grp", "ch")),
        P(("grp", "ch"), None),
        P(),
        P(),
        P(),
        P(None, "ch", None),
        P("ch", None),
        P(),
    )
    return jax.shard_map(
        functools.partial(shards, mesh.shape["grp"], mesh.shape["ch"]),
        mesh=mesh,
        in_specs=in_specs,
        out_specs=P(("grp", "ch"), None, None),
        check_vma=False,
    )
```

```python
import functools

import numpy as np

import jax
import jax.numpy as jnp
from jax import lax
from jax.experimental import pallas as pl
from jax.experimental.pallas import tpu as pltpu
from jax.sharding import PartitionSpec as P

MESH = pl.DeviceIdType.MESH
F32, BF16 = jnp.float32, jnp.bfloat16
STEPS = (-1, 0, 1)
OFFSETS = [(x, y, z) for x in STEPS for y in STEPS for z in STEPS]
PARTNERS = [(h, y, z) for h in (0, 1) for y in STEPS for z in STEPS if (h, y, z) != (0, 0, 0)]
PIECES = 3


def matmul_nt(left, right):
    return lax.dot_general(left, right, (((1,), (1,)), ((), ())), preferred_element_type=F32)


def rounded_gelu(value):
    scale = (2 / np.pi) ** 0.5
    half = 0.5 * value
    return (half + half * jnp.tanh(value * (scale + scale * 0.044715 * (value * value)))).astype(BF16)


def kernel(grps, n, feat_any, live_any, neigh_any, w1_any, w2_any, wm_any, wc_any, wp_any, wo_any, table_any, out, levels, mats, live, neigh, sems):
    g, m = lax.axis_index("grp"), lax.axis_index("ch")
    q = n // 2
    half, place_y = m // q, m % q
    slots, c0, voxels = feat_any.shape
    edge = round(voxels ** (1 / 3))
    c1 = wm_any.shape[2]

    def has(partner):
        _, y, z = partner
        return (place_y + y >= 0) & (place_y + y < q) & (g + z >= 0) & (g + z < grps)

    def coords(partner):
        h, y, z = partner
        return g + z, ((1 - half) if h else half) * q + place_y + y

    barrier = pltpu.get_barrier_semaphore()
    far = [p for p in PARTNERS if p[2] != 0]
    for p in sorted(far, key=lambda p: -sum(abs(s) for s in p)):

        @pl.when(has(p))
        def _():
            pl.semaphore_signal(barrier, inc=1, device_id=coords(p), device_id_type=MESH)

    for r in range(1, n):
        pl.semaphore_signal(barrier, inc=1, device_id=(g, (m + r) % n), device_id_type=MESH)

    (feat, w1, w2, wm, wo, wc, wp, b1, b2, f1, f2, bm, im_leaf, im_mid, table, gather, ext_leaf, planes, acc) = mats
    (local_sem, wsend, wrecv, hsend, hrecv) = sems
    for i, level in enumerate(levels):
        level.update(send=hsend, recv=hrecv.at[i % 2])
    loads = [
        pltpu.make_async_copy(source, target, local_sem.at[i])
        for i, (source, target) in enumerate(
            [(w1_any, w1), (w2_any, w2), (wm_any, wm), (wo_any, wo), (wc_any, wc.at[m % 2, m // 2, pl.ds(0, wc_any.shape[0])]), (wp_any, wp), (live_any, live), (neigh_any, neigh), (table_any, table), (feat_any, feat)]
        )
    ]
    for load in loads[-1:] + loads[:-1]:
        load.start()

    area = edge * edge

    def leaf_piece(level, partner):
        h, y, z = partner
        upper, right = (1 if z > 0 else 0), (1 if y > 0 else 0)
        far_side = 1 - half
        if z:
            if y:
                return level["send_l"].at[upper, right]
            if h:
                return level["send_z"].at[upper, pl.ds(pl.multiple_of(far_side * (area - edge), edge), edge)]
            return level["send_z"].at[upper]
        if not h:
            return level["send_y"].at[right]
        start, size = far_side * (edge - 1) * area + right * (area - edge if y else 0), edge if y else area
        return level["flat"].at[pl.ds(pl.multiple_of(start, edge), size)]

    def unpack(level, partner):
        index = PARTNERS.index(partner)
        value = level["land"][index][...].astype(F32)
        target = level["got"][index]
        target[...] = value.reshape(target.shape)
        return value

    def piece_of(level, partner):
        if "lines" in level:
            return leaf_piece(level, partner)
        if "rows" in level:
            return level["rows"]
        h, y, z = partner
        volume, caps = level["v"], level["caps"]
        length = volume.shape[0]
        pick_x = pl.ds((1 - half) * (length - 1), 1) if h else slice(None)
        pick_y = slice(None) if y == 0 else (pl.ds(length - 1, 1) if y > 0 else pl.ds(0, 1))
        if z == 0:
            return volume.at[pick_x, pick_y]
        return caps.at[1 if z > 0 else 0, pick_x, pick_y]

    def copy_to(level, index):
        h, y, z = PARTNERS[index]
        back = PARTNERS.index((h, -y, -z))
        return pltpu.make_async_remote_copy(
            src_ref=piece_of(level, PARTNERS[index]),
            dst_ref=level["got"].at[back] if "rows" in level else level.get("land", level["got"])[back],
            send_sem=level["send"].at[index],
            recv_sem=level["recv"].at[back],
            device_id=coords(PARTNERS[index]),
            device_id_type=MESH,
        )

    order = sorted(range(len(PARTNERS)), key=lambda i: -sum(abs(s) for s in PARTNERS[i]))

    def caps_of(level):
        volume, caps = level["v"], level["caps"]
        length = volume.shape[0]
        caps[0] = volume[:, :, 0:1, :]
        caps[1] = volume[:, :, length - 1 : length, :]

    def send(level):
        for i in order:

            @pl.when(has(PARTNERS[i]))
            def _():
                copy_to(level, i).start()

    order_of = [PARTNERS[i] for i in order]

    def sent(level):
        for i in order:

            @pl.when(has(PARTNERS[i]))
            def _():
                copy_to(level, i).wait_send()

    def wait_for(level, partners):
        for h, y, z in partners:

            @pl.when(has((h, -y, -z)))
            def _():
                copy_to(level, PARTNERS.index((h, y, z))).wait_recv()

    def receive(level):
        for i in order:
            h, y, z = PARTNERS[i]

            @pl.when(has((h, -y, -z)))
            def _():
                copy_to(level, i).wait_recv()

    def extend(level, own):
        volume, ext, caps = level["v"], level["ext"], level["caps"]
        length, lanes = volume.shape[0], volume.shape[3]
        middle = lanes // 2
        lane = lax.broadcasted_iota(jnp.int32, (1, 1, 1, lanes), 3)
        upper = (lane >= middle).astype(jnp.int32)
        if own:
            ext[1 : length + 1, 1 : length + 1, 1 : length + 1, :] = volume[...]
        firsts = {}
        for p in [(0, 0, 0)] + PARTNERS:
            a, b = coords(p)
            firsts[p] = jnp.where(has(p), (a * n + b) * 2, -8)

        def source_at(step):
            return slice(0, length) if step == 0 else (slice(0, 1) if step > 0 else slice(length - 1, length))

        def target_at(step):
            return slice(1, length + 1) if step == 0 else (slice(0, 1) if step < 0 else slice(length + 1, length + 2))

        for column, (x, y, z) in enumerate(OFFSETS):
            if (x, y, z) == (0, 0, 0):
                continue
            wanted = jnp.where(upper == 1, neigh[1, column], neigh[0, column])
            shape = tuple(length if s == 0 else 1 for s in (x, y, z)) + (lanes,)
            wanted = jnp.broadcast_to(wanted, shape)
            upper_full = jnp.broadcast_to(upper, shape)
            target = (target_at(x), target_at(y), target_at(z))
            value = jnp.zeros(shape, F32) if own else ext[target]
            for h in (0, 1) if x else (0,):
                for cy in (0, y) if y else (0,):
                    for cz in (0, z) if z else (0,):
                        p = (h, cy, cz)
                        if (p == (0, 0, 0)) != own:
                            continue
                        at_x = slice(0, 1) if h else source_at(x)
                        at_y = slice(0, 1) if cy else source_at(y)
                        at_z = slice(0, 1) if cz else source_at(z)
                        if p == (0, 0, 0):
                            if z:
                                found = caps[0 if z > 0 else 1, at_x, at_y, :, :]
                            else:
                                found = volume[at_x, at_y, at_z, :]
                        else:
                            found = level["got"][PARTNERS.index(p)][at_x, at_y, at_z, :]
                        swapped = jnp.concatenate([found[..., middle:], found[..., :middle]], axis=3)
                        value = jnp.where(
                            wanted == firsts[p] + upper_full,
                            found,
                            jnp.where(wanted == firsts[p] + 1 - upper_full, swapped, value),
                        )
            ext[target] = value

    half_lanes = slots * c0 // 2
    lane = lax.broadcasted_iota(jnp.int32, (edge, slots * c0), 1)
    block_of = (lane >= half_lanes).astype(jnp.int32)
    first_of = {}
    for p in [(0, 0, 0)] + PARTNERS:
        a, b = coords(p)
        first_of[p] = jnp.where(has(p), (a * n + b) * 2, -8)

    def choose(column, rows, sources, value=None):
        wanted = jnp.where(block_of == 1, neigh[1, column], neigh[0, column])
        owner = block_of
        if rows < edge:
            wanted, owner = wanted[:rows], owner[:rows]
        for p, found in sources:
            pieces = [found[r : r + min(rows, edge)] for r in range(0, rows, edge)]
            straight, crossed = wanted == first_of[p] + owner, wanted == first_of[p] + 1 - owner
            old = value if value is not None else [jnp.zeros_like(piece) for piece in pieces]
            value = [
                jnp.where(straight, piece, jnp.where(crossed, pltpu.roll(piece, half_lanes, 1), before))
                for piece, before in zip(pieces, old)
            ]
        return value

    def spots(plane, kind):
        axis, place = kind
        pitch = 2 * edge
        if axis == "face":
            return [(plane, slice((r + 1) * pitch + 1, (r + 1) * pitch + 1 + edge)) for r in range(edge)]
        if axis == "row":
            return [(plane, slice(place * pitch + 1, place * pitch + 1 + edge))]
        if axis == "column":
            return [(plane, pl.ds(pitch + place, edge, stride=pitch))]
        return [(plane, slice(place[0] * pitch + place[1], place[0] * pitch + place[1] + 1))]

    def put(plane, kind, column, rows, sources, add=False):
        where = spots(plane, kind)
        value = choose(column, rows, sources, [planes[spot] for spot in where] if add else None)
        for spot, part in zip(where, value):
            planes[spot] = part

    def add_plane(plane, weights, where):
        parts = []
        for i in range(3):
            for j in range(3):
                rows = [planes[plane, (r + i) * 2 * edge + j : (r + i) * 2 * edge + j + edge, :] for r in range(edge)]
                parts.append(jnp.concatenate(rows, axis=0).astype(BF16))
        update = matmul_nt(jnp.concatenate(parts, axis=1), weights)
        axis, at = where
        if axis == "x":
            acc[pl.ds(at, area), :] += update
            return
        for r in range(edge):
            rows = update[r * edge : (r + 1) * edge]
            if axis == "y":
                acc[r * area + at : r * area + at + edge, :] += rows
            else:
                acc[pl.ds(r * area + at, edge, stride=edge), :] += rows

    small = edge // 4
    cells = small**3

    def fill_gather():
        sub = lax.broadcasted_iota(jnp.int32, (8, gather.shape[1] // 3), 0)
        col = lax.broadcasted_iota(jnp.int32, (8, gather.shape[1] // 3), 1)
        width = sub.shape[1]
        entries = [neigh[b, d] * cells for b in range(slots) for d in range(27)] + list(range(cells))
        blocks = []
        for start in range(0, width, 8):
            block = jnp.zeros(sub.shape, jnp.int32)
            for s, entry in enumerate(entries[start : start + 8]):
                block = jnp.where(sub == s, entry, block)
            blocks.append(block.astype(F32))
        keys = jnp.dot(table[...], jnp.concatenate(blocks, axis=0).astype(BF16), preferred_element_type=F32)
        rows = slots * cells
        for k in range(3):
            offer = jnp.full(sub.shape, -1000, jnp.int32)
            for i, p in enumerate([(0, 0, 0)] + PARTNERS):
                at = i * rows - k * width
                offer = jnp.where((col >= at) & (col < at + rows), first_of[p] * cells + col - at, offer)
            offer = jnp.broadcast_to(offer[:1].astype(F32), keys.shape)
            gather[:, k * width : (k + 1) * width] = jnp.where(keys == offer, 1.0, 0.0).astype(BF16)

    def column_of(x, y, z):
        return 9 * (x + 1) + 3 * (y + 1) + z + 1

    def halo(level, weights, faces):
        volume, caps, lines = level["v"], level["caps"], level["lines"]
        got = {p: level["got"][i] for i, p in enumerate(PARTNERS)}
        last = edge - 1
        near = lambda s: 0 if s > 0 else last
        beyond = lambda s: 0 if s < 0 else edge + 1
        flag = lambda s: 0 if s > 0 else 1
        line_y = lambda y: slice(near(y) * edge, near(y) * edge + edge)
        skip = lambda start: pl.ds(start, edge, stride=edge)

        fresh = {}

        def arrive(partners):
            wait_for(level, partners)
            for p in partners:
                fresh[p] = unpack(level, p)

        arrive([(0, 0, -1), (0, 0, 1)])
        for z in (-1, 1):
            plane = 4 + (z > 0)
            sources = [((0, 0, 0), caps[flag(z)]), ((0, 0, z), fresh[0, 0, z])]
            put(plane, ("face", 0), column_of(0, 0, z), area, sources)
            add_plane(plane, faces[plane - 2], ("z", last - near(z)))
        arrive([(0, -1, 0), (0, 1, 0)] + [(0, y, z) for y in (-1, 1) for z in (-1, 1)])
        for y in (-1, 1):
            plane = 2 + (y > 0)
            flat = got[0, y, 0].reshape(edge * edge, slots * c0)
            own = volume[:, line_y(y), :].reshape(edge * edge, slots * c0)
            sources = [((0, 0, 0), own), ((0, y, 0), fresh[0, y, 0])]
            put(plane, ("face", 0), column_of(0, y, 0), area, sources)
            for z in (-1, 1):
                sources = [
                    ((0, 0, 0), lines[flag(z), flag(y)]),
                    ((0, y, 0), flat[skip(near(z)), :]),
                    ((0, 0, z), got[0, 0, z][skip(near(y)), :]),
                    ((0, y, z), fresh[0, y, z]),
                ]
                put(plane, ("column", beyond(z)), column_of(0, y, z), edge, sources)
            add_plane(plane, faces[plane - 2], ("y", (last - near(y)) * edge))
        for x in (-1, 1):
            plane, xe = (x > 0) + 0, near(x)
            put(plane, ("face", 0), column_of(x, 0, 0), area, [((0, 0, 0), volume[xe])])
            for y in (-1, 1):
                sources = [((0, 0, 0), volume[xe, line_y(y), :]), ((0, y, 0), got[0, y, 0][xe])]
                put(plane, ("row", beyond(y)), column_of(x, y, 0), edge, sources)
            for z in (-1, 1):
                span = slice(xe * edge, xe * edge + edge)
                sources = [((0, 0, 0), caps[flag(z), span, :]), ((0, 0, z), got[0, 0, z][span, :])]
                put(plane, ("column", beyond(z)), column_of(x, 0, z), edge, sources)
            for y in (-1, 1):
                for z in (-1, 1):
                    at = xe * edge + near(y)
                    sources = [
                        ((0, 0, 0), lines[flag(z), flag(y), xe : xe + 1, :]),
                        ((0, y, 0), got[0, y, 0][xe, near(z) : near(z) + 1, :]),
                        ((0, 0, z), got[0, 0, z][at : at + 1, :]),
                        ((0, y, z), got[0, y, z][xe : xe + 1, :]),
                    ]
                    put(plane, ("cell", (beyond(y), beyond(z))), column_of(x, y, z), 1, sources)
        add_plane(half, weights[2 * half], ("x", pl.multiple_of(half * last * area, area)))
        arrive([p for p in order_of[::-1] if p[0] == 1])
        plane = 1 - half
        x = 1 - 2 * half
        face = got[1, 0, 0]
        put(plane, ("face", 0), column_of(x, 0, 0), area, [((1, 0, 0), fresh[1, 0, 0])], True)
        for y in (-1, 1):
            sources = [((1, 0, 0), face[0, line_y(y), :]), ((1, y, 0), fresh[1, y, 0])]
            put(plane, ("row", beyond(y)), column_of(x, y, 0), edge, sources, True)
        for z in (-1, 1):
            sources = [((1, 0, 0), face[0, skip(near(z)), :]), ((1, 0, z), fresh[1, 0, z])]
            put(plane, ("column", beyond(z)), column_of(x, 0, z), edge, sources, True)
        for y in (-1, 1):
            for z in (-1, 1):
                at = near(y) * edge + near(z)
                sources = [
                    ((1, 0, 0), face[0, at : at + 1, :]),
                    ((1, y, 0), got[1, y, 0][0, near(z) : near(z) + 1, :]),
                    ((1, 0, z), got[1, 0, z][near(y) : near(y) + 1, :]),
                    ((1, y, z), got[1, y, z][pl.ds(half * last, 1), :]),
                ]
                put(plane, ("cell", (beyond(y), beyond(z))), column_of(x, y, z), 1, sources, True)
        add_plane(plane, weights[2 * plane], ("x", pl.multiple_of(plane * last * area, area)))

    def surface(level):
        volume, caps, lines = level["v"], level["caps"], level["lines"]
        for k, z in enumerate((0, edge - 1)):
            for x in range(edge):
                caps[k, x * edge : (x + 1) * edge, :] = volume[x, pl.ds(z, edge, stride=edge), :]
            for j, y in enumerate((0, edge - 1)):
                line = caps[k, pl.ds(y, edge, stride=edge), :]
                lines[k, j] = line
                level["send_l"][k, j] = line.astype(BF16)
            level["send_z"][k] = caps[k].astype(BF16)
        for j, y in enumerate((0, edge - 1)):
            face = volume[:, y * edge : (y + 1) * edge, :].reshape(area, slots * c0)
            level["send_y"][j] = face.astype(BF16)

    def fill_faces(weights, target):
        width = slots * c0
        for k in range(2):
            for i in range(3):
                target[k, :, 3 * i * width : 3 * (i + 1) * width] = weights[i, :, 6 * k * width : (6 * k + 3) * width]
                for j in range(3):
                    at, tap = (3 * i + j) * width, (3 * j + 2 * k) * width
                    target[2 + k, :, at : at + width] = weights[i, :, tap : tap + width]

    taps = wc.shape[2] - 1

    pairs = n // 2
    pair, core = m // 2, m % 2
    partner = pair * 2 + 1 - core

    def span(part):
        first, last = (taps + 1) * part // PIECES, (taps + 1) * (part + 1) // PIECES
        return pl.ds(first, last - first)

    def weight_copy(part, r, owner, target):
        return pltpu.make_async_remote_copy(
            src_ref=wc.at[core, owner, span(part)],
            dst_ref=wc.at[core, owner, span(part)],
            send_sem=wsend.at[part, r],
            recv_sem=wrecv.at[part, r],
            device_id=(g, target * 2 + core),
            device_id_type=MESH,
        )

    def share_copy(part, owner_core):
        return pltpu.make_async_remote_copy(
            src_ref=wc.at[owner_core, :, span(part)],
            dst_ref=wc.at[owner_core, :, span(part)],
            send_sem=wsend.at[part, 0],
            recv_sem=wrecv.at[part, 0],
            device_id=(g, partner),
            device_id_type=MESH,
        )

    def send_weights(part):
        for r in range(1, pairs):
            weight_copy(part, r, pair, (pair + r) % pairs).start()

    def hand_on(part):
        for r in range(1, pairs):
            other = (pair + pairs - r) % pairs
            weight_copy(part, r, other, other).wait_recv()
        share_copy(part, core).start()

    def diagonal(matrix):
        empty = jnp.zeros_like(matrix)
        return jnp.concatenate([matrix, empty], axis=1), jnp.concatenate([empty, matrix], axis=1)

    def fill_diagonal(weights, target):
        rows, width = weights.shape[1], 2 * weights.shape[2]
        for t in range(weights.shape[0]):
            top, bottom = diagonal(weights[t])
            at = (t % 9) * width
            target[t // 9, 0:rows, at : at + width] = top
            target[t // 9, rows : 2 * rows, at : at + width] = bottom

    def fill_upright(weights, target):
        rows, width = weights.shape[1:]
        for t in range(weights.shape[0]):
            empty = jnp.zeros((rows, width), BF16)
            for b in range(slots):
                at = (t % 9 * slots + b) * rows
                for other in range(slots):
                    there = weights[t] if other == b else empty
                    target[t // 9, at : at + rows, other * width : (other + 1) * width] = there

    def convolve_own(level, weights):
        lanes = slots * c0
        inside = slice(1, edge + 1)
        ext_leaf[inside, inside, inside, :] = level["v"][...].reshape(edge, edge, edge, lanes)
        for k in range(9):
            y, z = k // 3, k % 3
            rows = ext_leaf[:, y : y + edge, z : z + edge, :].reshape(edge + 2, edge * edge, lanes)
            im_leaf[:, :, k * lanes : (k + 1) * lanes] = rows.astype(BF16)
        total = None
        for x in range(3):
            window = im_leaf[x : x + edge].reshape(edge**3, 9 * lanes)
            term = matmul_nt(window, weights[x])
            total = term if total is None else total + term
        acc[...] = total

    leaf_a, leaf_b, mid, low = levels
    loads[-1].wait()
    packed = feat[...].reshape(slots * c0, voxels).astype(F32)
    turned = packed.T
    leaf_a["v"][...] = turned.reshape(edge, area, slots * c0)
    leaf_a["flat"][...] = turned.astype(BF16)
    surface(leaf_a)
    ext_leaf[...] = jnp.zeros_like(ext_leaf)
    planes[...] = jnp.zeros_like(planes)
    peers = n - 1
    for p in far:
        peers = peers + has(p).astype(jnp.int32)
    pl.semaphore_wait(barrier, peers)

    send(leaf_a)
    loads[4].wait()
    loads[5].wait()
    wc[core, pair, taps] = jnp.concatenate([wp[...]] * (c1 // c0), axis=1)
    send_weights(0)
    loads[0].wait()
    fill_diagonal(w1, b1)
    fill_faces(b1, f1)
    convolve_own(leaf_a, b1)
    loads[6].wait()
    loads[7].wait()
    loads[8].wait()
    fill_gather()
    sent(leaf_a)
    halo(leaf_a, b1, f1)
    first = rounded_gelu(acc[...])

    leaf_b["flat"][...] = first
    leaf_b["v"][...] = first.astype(F32).reshape(edge, area, slots * c0)
    surface(leaf_b)
    send(leaf_b)
    send_weights(1)
    loads[1].wait()
    fill_diagonal(w2, b2)
    fill_faces(b2, f2)
    convolve_own(leaf_b, b2)
    hand_on(0)
    sent(leaf_b)
    halo(leaf_b, b2, f2)
    second = rounded_gelu(acc[...])

    def halving(length):
        small = length // 2
        row = lax.broadcasted_iota(jnp.int32, (small**3, length**3), 0)
        column = lax.broadcasted_iota(jnp.int32, (small**3, length**3), 1)
        x, y, z = column // (length * length), column // length % length, column % length
        hit = row == (x // 2) * small * small + (y // 2) * small + z // 2
        return jnp.where(hit, 0.125, 0.0).astype(BF16)

    side = edge // 2
    pooled = jnp.dot(halving(edge), second, preferred_element_type=F32).astype(BF16).astype(F32)
    for x in range(side):
        for y in range(side):
            at = (x * side + y) * side
            mid["v"][x, y] = pooled[at : at + side]
    caps_of(mid)
    send(mid)
    send_weights(2)
    loads[2].wait()
    fill_upright(wm, bm)
    extend(mid, True)
    hand_on(1)
    sent(mid)
    receive(mid)
    extend(mid, False)
    lanes = slots * c0
    for k in range(9):
        ty, tz = k // 3, k % 3
        for y in range(side):
            im_mid[:, y * side : (y + 1) * side, k * lanes : (k + 1) * lanes] = mid["ext"][:, y + ty, tz : tz + side, :]
    total = None
    for x in range(3):
        window = im_mid[x : x + side].astype(BF16).reshape(side**3, 9 * lanes)
        term = jnp.dot(window, bm[x], preferred_element_type=F32)
        total = term if total is None else total + term
    middle = rounded_gelu(total)

    pooled = jnp.dot(halving(side), middle, preferred_element_type=F32)
    pooled = jnp.concatenate([pooled[:, b * c1 : (b + 1) * c1] for b in range(slots)], axis=0).astype(BF16)
    low["rows"][...] = pooled
    send(low)
    loads[3].wait()
    skip_top, skip_bottom = diagonal(wo[:, :c0])
    skip_weights = jnp.concatenate([skip_top, skip_bottom], axis=0)
    mixed = matmul_nt(skip_weights, second)
    hand_on(2)
    for part in range(PIECES):
        share_copy(part, 1 - core).wait_recv()
    c2 = n * wc.shape[3]
    rows = slots * cells
    project = lax.dot_general(
        wo[:, c0:], wc[:, :, taps].reshape(c2, c1)[:, :c0], (((1,), (1,)), ((), ())), preferred_element_type=F32
    )
    high = project.astype(BF16)
    project = jnp.concatenate([high, (project - high.astype(F32)).astype(BF16)], axis=0)
    row = lax.broadcasted_iota(jnp.int32, (3 * rows, voxels), 0) % cells
    column = lax.broadcasted_iota(jnp.int32, (3 * rows, voxels), 1)
    factor = edge // small
    x, y, z = column // area, column // edge % edge, column % edge
    widen = jnp.where(row == (x // factor) * small * small + (y // factor) * small + z // factor, 1.0, 0.0).astype(BF16)
    receive(low)
    sources = [pooled]
    for i, p in enumerate(PARTNERS):
        sources.append(jnp.where(has(p), low["got"][i], jnp.zeros_like(pooled)))
    spare = gather.shape[1] - len(sources) * slots * cells
    sources.append(jnp.zeros((spare, c1), BF16))
    spread = jnp.dot(gather[...], jnp.concatenate(sources, axis=0), preferred_element_type=F32).astype(BF16)
    window = jnp.concatenate([spread[t * rows : (t + 1) * rows] for t in range(taps)], axis=1)
    weights = jnp.concatenate([wc[:, :, t].reshape(c2, c1) for t in range(taps)], axis=1)
    hidden = rounded_gelu(matmul_nt(weights, jnp.concatenate([window] * 3, axis=0)))
    lifted = jnp.dot(project, hidden, preferred_element_type=F32)
    lifted = lifted[:c0] + lifted[c0:]
    high = lifted.astype(BF16).astype(F32)
    middle_bits = (lifted - high).astype(BF16).astype(F32)
    low_bits = lifted - high - middle_bits
    column = lax.broadcasted_iota(jnp.int32, lifted.shape, 1)
    terms = jnp.where(column < rows, high, jnp.where(column < 2 * rows, middle_bits, low_bits))
    owner_of = column % rows // cells
    terms = jnp.concatenate([jnp.where(owner_of == b, terms, 0.0) for b in range(slots)], axis=0).astype(BF16)
    mixed = mixed + jnp.dot(terms, widen, preferred_element_type=F32)
    owner = lax.broadcasted_iota(jnp.int32, mixed.shape, 0) // c0
    mixed = jnp.where(owner < live[0], mixed, 0.0).astype(BF16)
    for b in range(slots):
        out[b] = mixed[b * c0 : (b + 1) * c0]

    sent(low)
    for part in range(PIECES):
        share_copy(part, core).wait_send()
        for r in range(1, pairs):
            weight_copy(part, r, pair, (pair + r) % pairs).wait_send()


def leaf_scratch(length, lanes):
    def got(partner):
        h, y, z = partner
        if z == 0:
            return pltpu.VMEM((1 if h else length, length if y else length**2, lanes), F32)
        return pltpu.VMEM((length if h or y else length**2, lanes), F32)

    return dict(
        v=pltpu.VMEM((length, length**2, lanes), F32),
        caps=pltpu.VMEM((2, length**2, lanes), F32),
        lines=pltpu.VMEM((2, 2, length, lanes), F32),
        flat=pltpu.VMEM((length**3, lanes), BF16),
        send_y=pltpu.VMEM((2, length**2, lanes), BF16),
        send_z=pltpu.VMEM((2, length**2, lanes), BF16),
        send_l=pltpu.VMEM((2, 2, length, lanes), BF16),
        land=[pltpu.VMEM((length**2 if sum(map(abs, p)) == 1 else length, lanes), BF16) for p in PARTNERS],
        got=[got(p) for p in PARTNERS],
    )


def coarse_table(slots, small):
    cells = small**3
    table = np.zeros((len(OFFSETS) * slots * cells, 128), np.float32)
    row = 0
    for tap in OFFSETS:
        for b in range(slots):
            for cell in np.ndindex(small, small, small):
                there = np.array(cell) + np.array(tap)
                x, y, z = there // small + 1
                table[row, b * 27 + 9 * x + 3 * y + z] = 1
                x, y, z = there % small
                table[row, slots * 27 + (x * small + y) * small + z] = 1
                row += 1
    return jnp.asarray(table, BF16)


def level_scratch(length, lanes):
    def got(partner):
        h, y, z = partner
        return pltpu.VMEM((1 if h else length, 1 if y else length, 1 if z else length, lanes), F32)

    return dict(
        v=pltpu.VMEM((length, length, length, lanes), F32),
        caps=pltpu.VMEM((2, length, length, 1, lanes), F32),
        ext=pltpu.VMEM((length + 2,) * 3 + (lanes,), F32),
        got=[got(p) for p in PARTNERS],
    )


def shards(grps, n, features, live_counts, neighbours, w_first, w_second, w_middle, w_coarse, w_project, w_output):
    slots, c0, voxels = features.shape
    edge = round(voxels ** (1 / 3))
    w_middle = jnp.swapaxes(w_middle, 1, 2)
    taps, _, c1 = w_middle.shape
    lanes = slots * c0
    side, small = edge // 2, edge // 4
    levels = [
        leaf_scratch(edge, lanes),
        leaf_scratch(edge, lanes),
        level_scratch(side, lanes),
        dict(
            rows=pltpu.VMEM((slots * small**3, c1), BF16),
            got=pltpu.VMEM((len(PARTNERS), slots * small**3, c1), BF16),
        ),
    ]
    table = coarse_table(slots, small)
    mats = [
        pltpu.VMEM(features.shape, BF16),
        pltpu.VMEM(w_first.shape, BF16),
        pltpu.VMEM(w_second.shape, BF16),
        pltpu.VMEM(w_middle.shape, BF16),
        pltpu.VMEM(w_output.shape, BF16),
        pltpu.VMEM((2, n // 2, taps + 1) + w_coarse.shape[1:], BF16),
        pltpu.VMEM(w_project.shape, BF16),
        pltpu.VMEM((3, lanes, 9 * lanes), BF16),
        pltpu.VMEM((3, lanes, 9 * lanes), BF16),
        pltpu.VMEM((4, lanes, 9 * lanes), BF16),
        pltpu.VMEM((4, lanes, 9 * lanes), BF16),
        pltpu.VMEM((3, 9 * lanes, slots * c1), BF16),
        pltpu.VMEM((edge + 2, edge * edge, 9 * lanes), BF16),
        pltpu.VMEM((side + 2, side * side, 9 * lanes), F32),
        pltpu.VMEM(table.shape, BF16),
        pltpu.VMEM((table.shape[0], 3 * 128), BF16),
        pltpu.VMEM((edge + 2,) * 3 + (lanes,), F32),
        pltpu.VMEM((6, (edge + 2) * 2 * edge, lanes), F32),
        pltpu.VMEM((edge**3, lanes), F32),
    ]
    sems = [
        pltpu.SemaphoreType.DMA((10,)),
        pltpu.SemaphoreType.DMA((PIECES, n // 2)),
        pltpu.SemaphoreType.DMA((PIECES, n // 2)),
        pltpu.SemaphoreType.DMA((len(PARTNERS),)),
        pltpu.SemaphoreType.DMA((2, len(PARTNERS))),
    ]
    smem = pl.BlockSpec(memory_space=pltpu.SMEM)
    vmem = pl.BlockSpec(memory_space=pltpu.VMEM)
    stay = pl.BlockSpec(memory_space=pl.ANY)
    return pl.pallas_call(
        functools.partial(kernel, grps, n),
        out_shape=pltpu.VMEM(features.shape, BF16),
        in_specs=[stay] * 10,
        out_specs=vmem,
        scratch_shapes=[levels, mats, pltpu.SMEM(live_counts.shape, jnp.int32), pltpu.SMEM(neighbours.shape, jnp.int32), sems],
        compiler_params=pltpu.CompilerParams(collective_id=0, has_side_effects=True),
    )(features, live_counts, neighbours, w_first, w_second, w_middle, w_coarse, w_project, w_output, table)


def solution(mesh):
    in_specs = (
        P(("grp", "ch"), None, None),
        P(("grp", "ch")),
        P(("grp", "ch"), None),
        P(),
        P(),
        P(),
        P(None, "ch", None),
        P("ch", None),
        P(),
    )
    return jax.shard_map(
        functools.partial(shards, mesh.shape["grp"], mesh.shape["ch"]),
        mesh=mesh,
        in_specs=in_specs,
        out_specs=P(("grp", "ch"), None, None),
        check_vma=False,
    )
```
